32 devices in a mesh: member: 8 (over z, core), band: 4 (over y, x).
Axes of the slice: x: 2, y: 2, z: 4, core: 2. Of those that a mesh axis runs over, the one named last changes fastest.
Arguments:
- states: bfloat16 [16, 84, 64, 128], P('member', None, 'band'), may hold values from -6 to 6
- noise_field: float32 [16, 84, 64, 128], P('member', None, 'band'), may hold values from -3 to 3
- target: bfloat16 [84, 64, 128], P(None, 'band'), may hold values from -6 to 6
- w_conv: bfloat16 [512, 756], replicated, may hold values from -0.21875 to 0.21875
- w_proj: bfloat16 [84, 512], replicated, may hold values from -0.25 to 0.25
- matchings: int32 [4, 16], replicated, may hold values from 0 to 15, each once within a row
Outputs:
- grad_states: bfloat16 [16, 84, 64, 128], P('member', None, 'band')
- grad_conv: float32 [512, 756], P(('member', 'band'))
- grad_proj: float32 [84, 512], P(None, ('member', 'band'))
The draws below stay inside these ranges and needn't reach their ends.
Inputs may be any that keep to these rules, and one draw needn't show every extreme that they name: `matchings`: each row is a permutation of the 16 member numbers.
All inputs are finite; a program needn't handle non-finite values.
Results may differ from the reference program's by a relative error of at most 0.0075.
Values may be sent and summed in bfloat16 or wider, within the bound.
No kernel may reach another device: no remote copies, remote signals or barrier semaphores. Data moves between devices by JAX's collectives and lax.ppermute only.
A program may use at most 128 MiB of HBM per device.

```python
import math
import jax
import jax.numpy as jnp
from jax import lax

VARS = 84
HID = 512
MATCHES = 4
LON = 128
MEMBERS = 16
LAT = 64


def levels(rng, dims, cuts, smallest, high):
    gain, own = 1.0, jax.random.fold_in(rng, 6)
    for dim, shards_of in cuts:
        draws = jnp.exp(jax.random.uniform(jax.random.fold_in(own, dim), (shards_of,), jnp.float32, smallest / len(cuts), high / len(cuts)))
        gain = gain * jnp.repeat(draws, dims[dim] // shards_of).reshape([-1 if axis == dim else 1 for axis in range(len(dims))])
    return gain


def bell_draw(key, dims, deviation, limit, split=(), kind=jnp.bfloat16):
    result = deviation * jax.random.normal(key, dims, jnp.float32)
    if split:
        result = result * levels(key, dims, split, -0.22, 0.18)
    return jnp.clip(result, -limit, limit).astype(kind)


def setup_inputs(seed: int = 0) -> dict:
    splits = jax.random.split(jax.random.key(seed), 7)
    states = bell_draw(splits[0], (MEMBERS, VARS, LAT, LON), 1.0, 6.0, ((0, 8), (2, 4)))
    noise_field = bell_draw(splits[1], (MEMBERS, VARS, LAT, LON), 0.5, 3.0, ((0, 8), (2, 4)), jnp.float32)
    target = bell_draw(splits[2], (VARS, LAT, LON), 1.0, 6.0, ((1, 4),))
    w_conv = bell_draw(splits[3], (HID, 9 * VARS), (9 * VARS) ** -0.5, 0.21875)
    w_proj = bell_draw(splits[4], (VARS, HID), HID ** -0.5, 0.25)
    matchings = jax.vmap(lambda own: jax.random.permutation(own, MEMBERS))(jax.random.split(splits[5], MATCHES)).reshape((MATCHES, MEMBERS)).astype(jnp.int32)
    return dict(states=states, noise_field=noise_field, target=target, w_conv=w_conv, w_proj=w_proj, matchings=matchings)


SQRT_HALF = 0.7071067811865476
INV_ROOT_TWO_PI = 0.3989422804014327

def gelu_slope(preact):
    return 0.5 * (1.0 + lax.erf(preact * SQRT_HALF)) + preact * jnp.exp(-0.5 * preact * preact) * INV_ROOT_TWO_PI

def to_patches(values_in):
    leading = values_in.shape[:-3]
    channels, height, breadth = values_in.shape[-3:]
    n_lead = len(leading)
    blocks = values_in.reshape(leading + (channels, height // 8, 8, breadth // 4, 4))
    order = tuple(range(n_lead)) + (n_lead + 1, n_lead + 3, n_lead, n_lead + 2, n_lead + 4)
    blocks = jnp.transpose(blocks, order)
    return blocks.reshape(leading + (height // 8 * (breadth // 4), channels * 32))

def from_patches(values_in, channels, height, breadth):
    leading = values_in.shape[:-2]
    n_lead = len(leading)
    blocks = values_in.reshape(leading + (height // 8, breadth // 4, channels, 8, 4))
    order = tuple(range(n_lead)) + (n_lead + 2, n_lead, n_lead + 3, n_lead + 1, n_lead + 4)
    return jnp.transpose(blocks, order).reshape(leading + (channels, height, breadth))

def score_grad(differ):
    return differ * lax.rsqrt(lax.optimization_barrier(jnp.mean(differ * differ, axis=-1, keepdims=True)) + 1e-06)

def unfold(inputs_bf):
    channels, height, breadth = inputs_bf.shape
    padded = jnp.pad(inputs_bf, ((0, 0), (1, 1), (1, 1)))
    pieces = [padded[:, row_off:row_off + height, col_off:col_off + breadth] for row_off in range(3) for col_off in range(3)]
    return jnp.stack(pieces, axis=0).reshape(9 * channels, height * breadth)

def fold_back(grads):
    channels, height, breadth = grads.shape[1:]
    summed = jnp.zeros((channels, height + 2, breadth + 2), jnp.float32)
    for row_off in range(3):
        for col_off in range(3):
            summed = summed.at[:, row_off:row_off + height, col_off:col_off + breadth].add(grads[row_off * 3 + col_off])
    return summed[:, 1:-1, 1:-1]

def reference(states, noise_field, target, w_conv, w_proj, matchings):
    channels, height, breadth = states.shape[1:]
    count = matchings.shape[0]

    def prepare(states_m, noise_m):
        inputs_bf = (states_m.astype(jnp.float32) + noise_m).astype(jnp.bfloat16)
        columns = unfold(inputs_bf)
        preact = jnp.dot(w_conv, columns, preferred_element_type=jnp.float32)
        hidden = jax.nn.gelu(preact, approximate=False).astype(jnp.bfloat16)
        return (inputs_bf, columns, preact, hidden)

    def forward(item):
        inputs_bf, columns, preact, hidden = prepare(item[0], item[1])
        outputs = inputs_bf.astype(jnp.float32).reshape(channels, -1) + jnp.dot(w_proj, hidden, preferred_element_type=jnp.float32)
        return outputs.astype(jnp.bfloat16).reshape(channels, height, breadth)
    predicted = lax.map(forward, (states, noise_field))
    patches_all = to_patches(predicted)
    target_p = to_patches(target).astype(jnp.float32)
    numbers = jnp.broadcast_to(jnp.arange(MEMBERS, dtype=jnp.int32)[None, :], matchings.shape)
    inverse = jnp.zeros_like(matchings).at[jnp.arange(count, dtype=jnp.int32)[:, None], matchings].set(numbers)

    def member_grad(member):
        own_vals = patches_all[member].astype(jnp.float32)
        total = score_grad(own_vals - target_p)
        pair_sum = jnp.zeros_like(own_vals)
        for match in range(count):
            for lookup in (matchings, inverse):
                pair_sum = pair_sum + score_grad(own_vals - patches_all[lookup[match, member]].astype(jnp.float32))
        return (total - pair_sum / (2.0 * count)).astype(jnp.bfloat16)
    grads_p = lax.map(member_grad, jnp.arange(MEMBERS, dtype=jnp.int32))
    grad_pred = from_patches(grads_p, channels, height, breadth)

    def backward(carry, item):
        inputs_bf, columns, preact, hidden = prepare(item[0], item[1])
        grad_flat = item[2].reshape(channels, -1)
        dhidden = jnp.dot(w_proj.T, grad_flat, preferred_element_type=jnp.float32)
        grad_pre = (dhidden * gelu_slope(preact)).astype(jnp.bfloat16)
        conv_acc = carry[0] + jnp.dot(grad_pre, columns.T, preferred_element_type=jnp.float32)
        proj_acc = carry[1] + jnp.dot(grad_flat, hidden.T, preferred_element_type=jnp.float32)
        dcolumns = jnp.dot(w_conv.T, grad_pre, preferred_element_type=jnp.float32).reshape(9, channels, height, breadth)
        dinput = grad_flat.astype(jnp.float32).reshape(channels, height, breadth) + fold_back(dcolumns)
        return ((conv_acc, proj_acc), dinput.astype(jnp.bfloat16))
    start = (jnp.zeros(w_conv.shape, jnp.float32), jnp.zeros(w_proj.shape, jnp.float32))
    totals, grad_states = lax.scan(backward, start, (states, noise_field, grad_pred))
    factor = 1.0 / math.sqrt(MEMBERS * LAT * LON)
    return (grad_states, totals[0] * factor, totals[1] * factor)
```

```python
import functools

import jax
import jax.numpy as jnp
from jax import lax
from jax.experimental import pallas as pl
from jax.experimental.pallas import tpu as pltpu
from jax.sharding import PartitionSpec as P

SQRT_HALF = 0.7071067811865476
INV_ROOT_TWO_PI = 0.3989422804014327
F32 = jnp.float32
BF16 = jnp.bfloat16
LANES = 128
TAPS = 256
VMEM_LIMIT = 60 * 1024 * 1024


def vmem_params(count):
    return pltpu.CompilerParams(
        dimension_semantics=("arbitrary",) * count, vmem_limit_bytes=VMEM_LIMIT
    )


def shift_right(vals):
    lane = lax.broadcasted_iota(jnp.int32, vals.shape, 1)
    return jnp.where(lane == 0, 0.0, pltpu.roll(vals, 1, 1))


def shift_left(vals):
    width = vals.shape[1]
    lane = lax.broadcasted_iota(jnp.int32, vals.shape, 1)
    return jnp.where(lane == width - 1, 0.0, pltpu.roll(vals, width - 1, 1))


def expand_row(vals, scratch):
    channels = vals.shape[0]
    scratch[pl.ds(0, channels), :] = shift_right(vals)
    scratch[pl.ds(channels, channels), :] = vals
    scratch[pl.ds(2 * channels, channels), :] = shift_left(vals)
    return scratch[...].astype(BF16)


def regroup(rows, parts):
    channels, width = rows[0].shape
    size = width // parts
    lane = lax.broadcasted_iota(jnp.int32, (channels, width), 1) // size
    outs = []
    for q in range(parts):
        out = None
        for i in range(parts):
            moved = rows[i]
            shift = (i - q) * size % width
            if shift:
                moved = pltpu.roll(moved, shift, 1)
            out = moved if out is None else jnp.where(lane == i, moved, out)
        outs.append(out)
    return outs


class Sizes:
    def __init__(self, states, w_conv, member_count):
        self.mem, self.ch, self.lat, self.lon = states.shape
        self.hid = w_conv.shape[0]
        self.devs = member_count
        self.prows = self.lat // 8
        self.parts = member_count // self.prows
        self.groups = 8 // self.parts
        self.sub = self.groups * self.ch
        self.subpad = (self.sub + 7) // 8 * 8
        self.pos = self.lat * self.lon


def prep_kernel(sz, states, noise, target, w_conv, e_out, x_out, t_out, w_out, xs, es, ps):
    es[...] = jnp.zeros_like(es)
    x = (states[0].astype(F32) + noise[0]).astype(BF16)
    xs[...] = x.astype(F32).reshape(sz.ch * sz.lat, sz.lon)
    for row in range(sz.lat):
        vals = xs[pl.ds(row, sz.ch, stride=sz.lat), :]
        x_out[0, :, row * sz.lon : (row + 1) * sz.lon] = vals.astype(BF16)
        e_out[0, :, row * sz.lon : (row + 1) * sz.lon] = expand_row(vals, es)

    @pl.when(pl.program_id(0) == 0)
    def _():
        xs[...] = target[...].astype(F32).reshape(sz.ch * sz.lat, sz.lon)
        if sz.subpad > sz.sub:
            ps[...] = jnp.zeros_like(ps)
        for prow in range(sz.prows):
            for group in range(sz.groups):
                first = prow * 8 + group * sz.parts
                rows = [
                    xs[pl.ds(first + i, sz.ch, stride=sz.lat), :] for i in range(sz.parts)
                ]
                for q, out in enumerate(regroup(rows, sz.parts)):
                    ps[q, pl.ds(group * sz.ch, sz.ch), :] = out
            for q in range(sz.parts):
                t_out[prow * sz.parts + q] = ps[q].astype(BF16)

    @pl.when(pl.program_id(0) == sz.mem - 1)
    def _():
        taps = 3 * sz.ch
        for part in range(3):
            w_out[:, part * TAPS : (part + 1) * TAPS] = jnp.concatenate(
                [
                    w_conv[:, part * taps : (part + 1) * taps],
                    jnp.zeros((sz.hid, TAPS - taps), BF16),
                ],
                axis=1,
            )


def forward_kernel(sz, e_in, x_in, halo_up, halo_dn, w3, w_proj, hid_out, slope_out, snd, ext, es, ps):
    width = sz.lon
    prow = pl.program_id(1)

    @pl.when(prow == 0)
    def _():
        es[...] = jnp.zeros_like(es)
        if sz.subpad > sz.sub:
            ps[...] = jnp.zeros_like(ps)
        ext[:, width : width + sz.pos] = e_in[0]
        ext[:, 0:width] = expand_row(halo_up[0, :, 0, :].astype(F32), es)
        ext[:, width + sz.pos :] = expand_row(halo_dn[0, :, 0, :].astype(F32), es)

    base = prow * (8 * width)
    rows = []
    for pair in range(4):
        start = pl.multiple_of(base + pair * 2 * width, width)
        cols = jnp.concatenate(
            [ext[:, pl.ds(pl.multiple_of(start + ro * width, width), 2 * width)] for ro in range(3)],
            axis=0,
        )
        preact = jnp.dot(w3[...], cols, preferred_element_type=F32)
        cdf = 0.5 + 0.5 * lax.erf(preact * SQRT_HALF)
        hidden = (preact * cdf).astype(BF16)
        bell = jnp.exp(preact * preact * (-0.5))
        here = slice(pair * 2 * width, (pair + 1) * 2 * width)
        hid_out[0, :, here] = hidden
        slope_out[0, :, here] = cdf + preact * (bell * INV_ROOT_TWO_PI)
        pred = x_in[0, :, here].astype(F32) + jnp.dot(
            w_proj[...], hidden, preferred_element_type=F32
        )
        pred = pred.astype(BF16).astype(F32)
        rows += [pred[:, :width], pred[:, width:]]
    for group in range(sz.groups):
        outs = regroup(rows[group * sz.parts : (group + 1) * sz.parts], sz.parts)
        for q, out in enumerate(outs):
            ps[q, pl.ds(group * sz.ch, sz.ch), :] = out
    for q in range(sz.parts):
        snd[q, 0] = ps[q].astype(BF16)


def pair_kernel(sz, count, members, match, device, preds, truth, grads, vals, tsc, sums, scale, inv):
    norm = 1.0 / (32.0 * sz.ch)
    vals[...] = preds[...].reshape(members, sz.subpad, LANES).astype(F32)
    tsc[...] = truth[0].astype(F32)
    folds = sz.subpad // 8

    def squares(diff):
        return jnp.sum((diff * diff).reshape(folds, 8, LANES), axis=0)

    def first(m, carry):
        own = vals[m]
        sums[pl.ds(pl.multiple_of((count * members + m) * 8, 8), 8), :] = squares(own - tsc[...])
        for k in range(count):
            other = match[k, m]
            inv[k, other] = m
            at = pl.multiple_of((k * members + m) * 8, 8)
            sums[pl.ds(at, 8), :] = squares(own - vals[other])
        return carry

    lax.fori_loop(0, members, first, 0)
    rows = (count + 1) * members
    total = sums[pl.ds(0, rows, stride=8), :]
    for j in range(1, 8):
        total = total + sums[pl.ds(j, rows, stride=8), :]
    size = sz.lon // sz.parts
    step = size
    while step < LANES:
        total = total + pltpu.roll(total, step, 1)
        step *= 2
    lane = lax.broadcasted_iota(jnp.int32, total.shape, 1)
    for bit in (1, 2):
        total = total + jnp.where(
            (lane & bit) == 0, pltpu.roll(total, LANES - bit, 1), pltpu.roll(total, bit, 1)
        )
    scale[...] = lax.rsqrt(total * norm + 1e-06)

    def second(m, carry):
        own = vals[m]

        def term(other, index):
            return (own - other) * scale[pl.ds(index, 1), :]

        acc = jnp.zeros_like(own)
        for k in range(count):
            acc = acc + term(vals[match[k, m]], k * members + m)
            back = inv[k, m]
            acc = acc + term(vals[back], k * members + back)
        out = term(tsc[...], count * members + m) - acc / (2.0 * count)
        grads[m // sz.mem, m % sz.mem] = out.astype(BF16)
        return carry

    lax.fori_loop(0, members, second, 0)


def weight_kernel(sz, back, hid, slope, e_in, halo_up, halo_dn, w_proj_t, wt3, gp_out, gpre_out, wg_out, edge_out, ext, es, rows_f, acc):
    width = sz.lon
    member = pl.program_id(0)
    es[...] = jnp.zeros_like(es)
    ext[:, width : width + sz.pos] = e_in[0]
    ext[:, 0:width] = expand_row(halo_up[0, :, 0, :].astype(F32), es)
    ext[:, width + sz.pos :] = expand_row(halo_dn[0, :, 0, :].astype(F32), es)
    for prow in range(sz.prows):
        for q in range(sz.parts):
            rows_f[q] = back[prow * sz.parts + q, 0].astype(F32)
        for group in range(sz.groups):
            outs = regroup(
                [rows_f[q, pl.ds(group * sz.ch, sz.ch), :] for q in range(sz.parts)], sz.parts
            )
            for i, out in enumerate(outs):
                row = prow * 8 + group * sz.parts + i
                gp_out[0, :, row * width : (row + 1) * width] = out.astype(BF16)
    zero = jnp.zeros((sz.hid, width), BF16)
    gpre_out[0, :, 0:width] = zero
    gpre_out[0, :, width + sz.pos :] = zero
    for pair in range(sz.lat // 2):
        here = slice(pair * 2 * width, (pair + 1) * 2 * width)
        dhid = jnp.dot(w_proj_t[...], gp_out[0, :, here], preferred_element_type=F32)
        there = slice((pair * 2 + 1) * width, (pair * 2 + 3) * width)
        gpre_out[0, :, there] = (dhid * slope[0, :, here]).astype(BF16)
    gpre = gpre_out[0, :, width : width + sz.pos]
    dims = (((1,), (1,)), ((), ()))
    for ro in range(4):
        if ro < 3:
            term = lax.dot_general(
                gpre, ext[:, ro * width : ro * width + sz.pos], dims, preferred_element_type=F32
            )
            at = slice(ro * TAPS, (ro + 1) * TAPS)
        else:
            term = lax.dot_general(hid[0], gp_out[0], dims, preferred_element_type=F32)
            at = slice(3 * TAPS, 3 * TAPS + sz.ch)

        @pl.when(member == 0)
        def _():
            acc[:, at] = term

        @pl.when(member > 0)
        def _():
            acc[:, at] = acc[:, at] + term

    for side in range(2):
        col = 0 if side == 0 else sz.pos - width
        part = jnp.dot(
            wt3[0 if side == 0 else 2], gpre[:, col : col + width], preferred_element_type=F32
        )
        edge_out[0, side] = fold_taps(part, sz.ch)

    @pl.when(member == sz.mem - 1)
    def _():
        wg_out[:, : 3 * TAPS + sz.ch] = acc[...].astype(BF16)
        wg_out[:, 3 * TAPS + sz.ch :] = jnp.zeros(
            (sz.hid, wg_out.shape[1] - 3 * TAPS - sz.ch), BF16
        )


def fold_taps(part, channels):
    return (
        part[channels : 2 * channels]
        + shift_left(part[0:channels])
        + shift_right(part[2 * channels : 3 * channels])
    )


def data_kernel(sz, gpre, gp, wt3, from_dn, from_up, out, gs):
    width = sz.lon
    for pair in range(sz.lat // 2):
        part = None
        for ro in range(3):
            start = (pair * 2 + 2 - ro) * width
            term = jnp.dot(
                wt3[ro], gpre[0, :, start : start + 2 * width], preferred_element_type=F32
            )
            part = term if part is None else part + term
        for i in range(2):
            row = pair * 2 + i
            total = gp[0, :, row * width : (row + 1) * width].astype(F32) + fold_taps(
                part[:, i * width : (i + 1) * width], sz.ch
            )
            if row == 0:
                total = total + from_up[0, 0]
            if row == sz.lat - 1:
                total = total + from_dn[0, 0]
            gs[pl.ds(row, sz.ch, stride=sz.lat), :] = total
    out[0] = gs[...].reshape(sz.ch, sz.lat, width).astype(BF16)


def spec(shape, index):
    return pl.BlockSpec(shape, index)


def whole(shape):
    return pl.BlockSpec(shape, lambda *_: (0,) * len(shape))


def on_device(states, noise_field, target, w_conv, w_proj, matchings):
    member_count = lax.axis_size("member")
    band_count = lax.axis_size("band")
    sz = Sizes(states, w_conv, member_count)
    mem, ch, lat, lon, hid, pos = sz.mem, sz.ch, sz.lat, sz.lon, sz.hid, sz.pos
    count = matchings.shape[0]
    members = mem * member_count
    down = [(i, i + 1) for i in range(band_count - 1)]
    up = [(i + 1, i) for i in range(band_count - 1)]

    def edge(row):
        return (
            states[:, :, row : row + 1].astype(F32) + noise_field[:, :, row : row + 1]
        ).astype(BF16)

    halo_up = lax.ppermute(edge(lat - 1), "band", down)
    halo_dn = lax.ppermute(edge(0), "band", up)

    def by_member(*shape):
        return spec((1,) + shape, lambda m, *_: (m,) + (0,) * len(shape))

    e_in, x_in, truth, w3 = pl.pallas_call(
        functools.partial(prep_kernel, sz),
        grid=(mem,),
        in_specs=[
            by_member(ch, lat, lon),
            by_member(ch, lat, lon),
            whole((ch, lat, lon)),
            whole(w_conv.shape),
        ],
        out_specs=[
            by_member(TAPS, pos),
            by_member(ch, pos),
            whole((sz.devs, sz.subpad, LANES)),
            whole((hid, 3 * TAPS)),
        ],
        out_shape=[
            jax.ShapeDtypeStruct((mem, TAPS, pos), BF16),
            jax.ShapeDtypeStruct((mem, ch, pos), BF16),
            jax.ShapeDtypeStruct((sz.devs, sz.subpad, LANES), BF16),
            jax.ShapeDtypeStruct((hid, 3 * TAPS), BF16),
        ],
        scratch_shapes=[
            pltpu.VMEM((ch * lat, lon), F32),
            pltpu.VMEM((TAPS, lon), F32),
            pltpu.VMEM((sz.parts, sz.subpad, LANES), F32),
        ],
        compiler_params=vmem_params(1),
        cost_estimate=pl.CostEstimate(flops=10_000_000, bytes_accessed=8_000_000, transcendentals=0),
        name="prep",
    )(states, noise_field, target, w_conv)

    hidden, slope, snd = pl.pallas_call(
        functools.partial(forward_kernel, sz),
        grid=(mem, sz.prows),
        in_specs=[
            spec((1, TAPS, pos), lambda m, p: (m, 0, 0)),
            spec((1, ch, 8 * lon), lambda m, p: (m, 0, p)),
            spec((1, ch, 1, lon), lambda m, p: (m, 0, 0, 0)),
            spec((1, ch, 1, lon), lambda m, p: (m, 0, 0, 0)),
            whole((hid, 3 * TAPS)),
            whole(w_proj.shape),
        ],
        out_specs=[
            spec((1, hid, 8 * lon), lambda m, p: (m, 0, p)),
            spec((1, hid, 8 * lon), lambda m, p: (m, 0, p)),
            spec((sz.parts, 1, sz.subpad, LANES), lambda m, p: (p, m, 0, 0)),
        ],
        out_shape=[
            jax.ShapeDtypeStruct((mem, hid, pos), BF16),
            jax.ShapeDtypeStruct((mem, hid, pos), F32),
            jax.ShapeDtypeStruct((sz.devs, mem, sz.subpad, LANES), BF16),
        ],
        scratch_shapes=[
            pltpu.VMEM((TAPS, pos + 2 * lon), BF16),
            pltpu.VMEM((TAPS, lon), F32),
            pltpu.VMEM((sz.parts, sz.subpad, LANES), F32),
        ],
        compiler_params=vmem_params(2),
        cost_estimate=pl.CostEstimate(flops=4_000_000_000, bytes_accessed=18_000_000, transcendentals=4_000_000),
        name="forward",
    )(e_in, x_in, halo_up, halo_dn, w3, w_proj)

    preds = lax.all_to_all(snd, "member", 0, 0, tiled=True)

    device = lax.axis_index("member").astype(jnp.int32).reshape(1)
    rows = (count + 1) * members
    grads = pl.pallas_call(
        functools.partial(pair_kernel, sz, count, members),
        grid_spec=pltpu.PrefetchScalarGridSpec(
            num_scalar_prefetch=2,
            grid=(1,),
            in_specs=[
                whole((sz.devs, mem, sz.subpad, LANES)),
                spec((1, sz.subpad, LANES), lambda i, match, device: (device[0], 0, 0)),
            ],
            out_specs=whole((sz.devs, mem, sz.subpad, LANES)),
            scratch_shapes=[
                pltpu.VMEM((members, sz.subpad, LANES), F32),
                pltpu.VMEM((sz.subpad, LANES), F32),
                pltpu.VMEM((rows * 8, LANES), F32),
                pltpu.VMEM((rows, LANES), F32),
                pltpu.SMEM((count, members), jnp.int32),
            ],
        ),
        out_shape=jax.ShapeDtypeStruct((sz.devs, mem, sz.subpad, LANES), BF16),
        compiler_params=vmem_params(1),
        name="pairs",
    )(matchings, device, preds, truth)

    back = lax.all_to_all(grads, "member", 0, 0, tiled=True)

    w_proj_t = w_proj.T
    wt3 = jnp.pad(w_conv.T.reshape(3, 3 * ch, hid), ((0, 0), (0, TAPS - 3 * ch), (0, 0)))
    cols = 4 * TAPS - LANES
    grad_pred, grad_pre, partial, edges = pl.pallas_call(
        functools.partial(weight_kernel, sz),
        grid=(mem,),
        in_specs=[
            spec((sz.devs, 1, sz.subpad, LANES), lambda m: (0, m, 0, 0)),
            by_member(hid, pos),
            by_member(hid, pos),
            by_member(TAPS, pos),
            by_member(ch, 1, lon),
            by_member(ch, 1, lon),
            whole(w_proj_t.shape),
            whole(wt3.shape),
        ],
        out_specs=[
            by_member(ch, pos),
            by_member(hid, pos + 2 * lon),
            whole((hid, cols)),
            by_member(2, ch, lon),
        ],
        out_shape=[
            jax.ShapeDtypeStruct((mem, ch, pos), BF16),
            jax.ShapeDtypeStruct((mem, hid, pos + 2 * lon), BF16),
            jax.ShapeDtypeStruct((hid, cols), BF16),
            jax.ShapeDtypeStruct((mem, 2, ch, lon), F32),
        ],
        scratch_shapes=[
            pltpu.VMEM((TAPS, pos + 2 * lon), BF16),
            pltpu.VMEM((TAPS, lon), F32),
            pltpu.VMEM((sz.parts, sz.subpad, LANES), F32),
            pltpu.VMEM((hid, 3 * TAPS + ch), F32),
        ],
        compiler_params=vmem_params(1),
        name="weights",
    )(back, hidden, slope, e_in, halo_up, halo_dn, w_proj_t, wt3)

    shards = member_count * band_count
    terms = lax.all_to_all(
        partial.reshape(shards, hid // shards, cols), ("member", "band"), 0, 0, tiled=True
    )
    from_dn = lax.ppermute(edges[:, 0:1], "band", up)
    from_up = lax.ppermute(edges[:, 1:2], "band", down)

    grad_states = pl.pallas_call(
        functools.partial(data_kernel, sz),
        grid=(mem,),
        in_specs=[
            by_member(hid, pos + 2 * lon),
            by_member(ch, pos),
            whole(wt3.shape),
            by_member(1, ch, lon),
            by_member(1, ch, lon),
        ],
        out_specs=by_member(ch, lat, lon),
        out_shape=jax.ShapeDtypeStruct((mem, ch, lat, lon), BF16),
        scratch_shapes=[pltpu.VMEM((ch * lat, lon), F32)],
        compiler_params=vmem_params(1),
        cost_estimate=pl.CostEstimate(flops=4_000_000_000, bytes_accessed=8_000_000, transcendentals=0),
        name="data",
    )(grad_pre, grad_pred, wt3, from_dn, from_up)

    factor = 1.0 / (pos * members * band_count) ** 0.5
    total = jnp.sum(terms.astype(F32), axis=0) * factor
    own = hid // shards
    grad_conv = total[:, : 3 * TAPS].reshape(own, 3, TAPS)[:, :, : 3 * ch].reshape(own, 9 * ch)
    grad_proj = total[:, 3 * TAPS : 3 * TAPS + ch].T
    return grad_states, grad_conv, grad_proj


def solution(mesh):
    return jax.shard_map(
        on_device,
        mesh=mesh,
        in_specs=(
            P("member", None, "band", None),
            P("member", None, "band", None),
            P(None, "band", None),
            P(),
            P(),
            P(),
        ),
        out_specs=(
            P("member", None, "band", None),
            P(("member", "band"), None),
            P(None, ("member", "band")),
        ),
        check_vma=False,
    )
```

```python
import functools

import jax
import jax.numpy as jnp
from jax import lax
from jax.experimental import pallas as pl
from jax.experimental.pallas import tpu as pltpu
from jax.sharding import PartitionSpec as P

SQRT_HALF = 0.7071067811865476
INV_ROOT_TWO_PI = 0.3989422804014327
F32 = jnp.float32
BF16 = jnp.bfloat16
LANES = 128
TAPS = 256
VMEM_LIMIT = 60 * 1024 * 1024


def vmem_params(count):
    return pltpu.CompilerParams(
        dimension_semantics=("arbitrary",) * count, vmem_limit_bytes=VMEM_LIMIT
    )


def shift_right(vals):
    lane = lax.broadcasted_iota(jnp.int32, vals.shape, 1)
    return jnp.where(lane == 0, 0.0, pltpu.roll(vals, 1, 1))


def shift_left(vals):
    width = vals.shape[1]
    lane = lax.broadcasted_iota(jnp.int32, vals.shape, 1)
    return jnp.where(lane == width - 1, 0.0, pltpu.roll(vals, width - 1, 1))


def expand_row(vals, scratch):
    channels = vals.shape[0]
    scratch[pl.ds(0, channels), :] = shift_right(vals)
    scratch[pl.ds(channels, channels), :] = vals
    scratch[pl.ds(2 * channels, channels), :] = shift_left(vals)
    return scratch[...].astype(BF16)


def swap_blocks(rows):
    parts = len(rows)
    size = rows[0].shape[1] // parts
    lane = lax.broadcasted_iota(jnp.int32, rows[0].shape, 1)
    rows = list(rows)
    bit = 1
    while bit < parts:
        low = (lane & (bit * size)) == 0
        shift = bit * size
        width = rows[0].shape[1]
        for i in range(parts):
            if i & bit:
                continue
            a, b = rows[i], rows[i | bit]
            rows[i] = jnp.where(low, a, pltpu.roll(b, shift, 1))
            rows[i | bit] = jnp.where(low, pltpu.roll(a, width - shift, 1), b)
        bit *= 2
    return rows


class Sizes:
    def __init__(self, states, w_conv, member_count):
        self.mem, self.ch, self.lat, self.lon = states.shape
        self.hid = w_conv.shape[0]
        self.devs = member_count
        prows = self.lat // 8
        self.chunks = prows if member_count <= 8 else 1
        self.crows = self.lat // self.chunks
        self.parts = self.devs * 8 // self.crows
        self.cpos = self.crows * self.lon
        self.sub = self.mem * self.ch
        self.chpad = (self.ch + 7) // 8 * 8
        self.pos = self.lat * self.lon
        assert self.parts == 8 and self.crows % 8 == 0


def prep_kernel(sz, states, noise, target, w_conv, e_out, x_out, t_out, w_out, xs, es):
    es[...] = jnp.zeros_like(es)
    x = (states[0].astype(F32) + noise[0]).astype(BF16)
    xs[...] = x.astype(F32).reshape(sz.ch * sz.lat, sz.lon)
    for row in range(sz.lat):
        vals = xs[pl.ds(row, sz.ch, stride=sz.lat), :]
        x_out[0, :, row * sz.lon : (row + 1) * sz.lon] = vals.astype(BF16)
        e_out[0, :, row * sz.lon : (row + 1) * sz.lon] = expand_row(vals, es)

    @pl.when(pl.program_id(0) == 0)
    def _():
        xs[...] = target[...].astype(F32).reshape(sz.ch * sz.lat, sz.lon)
        for chunk in range(sz.chunks):
            for prow in range(sz.crows // 8):
                first = chunk * sz.crows + prow * 8
                rows = [xs[pl.ds(first + i, sz.ch, stride=sz.lat), :] for i in range(8)]
                for q, out in enumerate(swap_blocks(rows)):
                    t_out[chunk, prow * 8 + q] = out.astype(BF16)

    @pl.when(pl.program_id(0) == sz.mem - 1)
    def _():
        taps = 3 * sz.ch
        for part in range(3):
            w_out[:, part * TAPS : (part + 1) * TAPS] = jnp.concatenate(
                [
                    w_conv[:, part * taps : (part + 1) * taps],
                    jnp.zeros((sz.hid, TAPS - taps), BF16),
                ],
                axis=1,
            )


def extend(sz, chunk, ext, es, e_in, halo_up, halo_dn):
    width = sz.lon
    first = chunk * sz.crows
    last = first + sz.crows
    es[...] = jnp.zeros_like(es)
    low = max(first - 1, 0)
    high = min(last + 1, sz.lat)
    at = (low - first + 1) * width
    ext[:, at : at + (high - low) * width] = e_in[0, :, low * width : high * width]
    if first == 0:
        ext[:, 0:width] = expand_row(halo_up[0, :, 0, :].astype(F32), es)
    if last == sz.lat:
        ext[:, width + sz.cpos :] = expand_row(halo_dn[0, :, 0, :].astype(F32), es)


def forward_kernel(sz, chunk, e_in, x_in, halo_up, halo_dn, w3, w_proj, hid_out, slope_out, snd, ext, es, ps):
    width = sz.lon
    member = pl.program_id(0)
    extend(sz, chunk, ext, es, e_in, halo_up, halo_dn)
    rows = []
    for pair in range(sz.crows // 2):
        cols = jnp.concatenate(
            [ext[:, (pair * 2 + ro) * width : (pair * 2 + ro + 2) * width] for ro in range(3)], axis=0
        )
        preact = jnp.dot(w3[...], cols, preferred_element_type=F32)
        twice = 1.0 + lax.erf(preact * SQRT_HALF)
        hidden = (preact * twice).astype(BF16)
        bell = jnp.exp(preact * preact * (-0.5)) * (2.0 * INV_ROOT_TWO_PI)
        here = slice(pair * 2 * width, (pair + 1) * 2 * width)
        hid_out[0, :, here] = hidden
        slope_out[0, :, here] = (twice + preact * bell).astype(BF16)
        pred = x_in[0, :, here].astype(F32) + jnp.dot(
            w_proj[...], hidden, preferred_element_type=F32
        )
        pred = pred.astype(BF16).astype(F32)
        rows += [pred[:, :width], pred[:, width:]]
    for prow in range(sz.crows // 8):
        for q, out in enumerate(swap_blocks(rows[prow * 8 : (prow + 1) * 8])):
            for m in range(sz.mem):

                @pl.when(member == m)
                def _():
                    ps[prow * 8 + q, pl.ds(m * sz.ch, sz.ch), :] = out

    @pl.when(member == sz.mem - 1)
    def _():
        snd[...] = ps[...].astype(BF16)


def pair_kernel(sz, count, match, device, preds, truth, grads, vals, tsc, sums, scale, gs, inv):
    norm = 1.0 / (32.0 * sz.ch)
    members = sz.devs * sz.mem
    ch, folds = sz.ch, sz.chpad // 8
    tail = folds * 8 - 8
    tsc[pl.ds(tail, 8), :] = jnp.zeros((8, LANES), F32)
    tsc[pl.ds(0, ch), :] = truth[0, 0].astype(F32)

    def unpack(src, carry):
        gs[...] = preds[src].astype(F32)
        for j in range(sz.mem):
            vals[src * sz.mem + j, pl.ds(tail, 8), :] = jnp.zeros((8, LANES), F32)
            vals[src * sz.mem + j, pl.ds(0, ch), :] = gs[pl.ds(j * ch, ch), :]
        return carry

    lax.fori_loop(0, sz.devs, unpack, 0)

    def squares(diff):
        return jnp.sum((diff * diff).reshape(folds, 8, LANES), axis=0)

    def first(m, carry):
        own = vals[m]
        sums[pl.ds(pl.multiple_of((count * members + m) * 8, 8), 8), :] = squares(own - tsc[...])
        for k in range(count):
            other = match[k, m]
            inv[k, other] = m
            at = pl.multiple_of((k * members + m) * 8, 8)
            sums[pl.ds(at, 8), :] = squares(own - vals[other])
        return carry

    lax.fori_loop(0, members, first, 0)
    rows = (count + 1) * members
    total = sums[pl.ds(0, rows, stride=8), :]
    for j in range(1, 8):
        total = total + sums[pl.ds(j, rows, stride=8), :]
    step = sz.lon // sz.parts
    while step < LANES:
        total = total + pltpu.roll(total, step, 1)
        step *= 2
    lane = lax.broadcasted_iota(jnp.int32, total.shape, 1)
    for bit in (1, 2):
        total = total + jnp.where(
            (lane & bit) == 0, pltpu.roll(total, LANES - bit, 1), pltpu.roll(total, bit, 1)
        )
    scale[...] = lax.rsqrt(total * norm + 1e-06)

    def second(src, carry):
        for j in range(sz.mem):
            m = src * sz.mem + j
            own = vals[m]

            def term(other, index):
                return (own - other) * scale[pl.ds(index, 1), :]

            acc = None
            for k in range(count):
                back = inv[k, m]
                both = term(vals[match[k, m]], k * members + m)
                both = both + term(vals[back], k * members + back)
                acc = both if acc is None else acc + both
            out = term(tsc[...], count * members + m) - acc * (0.5 / count)
            gs[pl.ds(j * ch, ch), :] = out[:ch]
        grads[src] = gs[...].astype(BF16)
        return carry

    lax.fori_loop(0, sz.devs, second, 0)


def fold_taps(part, channels):
    return (
        part[channels : 2 * channels]
        + shift_left(part[0:channels])
        + shift_right(part[2 * channels : 3 * channels])
    )


def weight_kernel(sz, chunk, *refs):
    refs = list(refs)
    back, hid, slope, e_in, halo_up, halo_dn, w_proj_t, wt3 = refs[:8]
    refs = refs[8:]
    acc_in = refs.pop(0) if chunk else None
    gp_out, gpre_out, wg_out, edge_out, ext, es, rows_f, acc = refs
    width = sz.lon
    member = pl.program_id(0)
    final = chunk == sz.chunks - 1
    extend(sz, chunk, ext, es, e_in, halo_up, halo_dn)
    for prow in range(sz.crows // 8):
        for q in range(8):
            rows_f[q] = back[prow * 8 + q].astype(F32)
        for m in range(sz.mem):

            @pl.when(member == m)
            def _():
                outs = swap_blocks([rows_f[q, pl.ds(m * sz.ch, sz.ch), :] for q in range(8)])
                for i, out in enumerate(outs):
                    row = prow * 8 + i
                    gp_out[0, :, row * width : (row + 1) * width] = out.astype(BF16)

    for pair in range(sz.crows // 2):
        here = slice(pair * 2 * width, (pair + 1) * 2 * width)
        dhid = jnp.dot(w_proj_t[...], gp_out[0, :, here], preferred_element_type=F32)
        gpre_out[0, :, here] = (dhid * slope[0, :, here].astype(F32)).astype(BF16)
    gpre = gpre_out[0]
    dims = (((1,), (1,)), ((), ()))
    for ro in range(4):
        if ro < 3:
            term = lax.dot_general(
                gpre, ext[:, ro * width : ro * width + sz.cpos], dims, preferred_element_type=F32
            )
            at = slice(ro * TAPS, (ro + 1) * TAPS)
        else:
            term = lax.dot_general(hid[0], gp_out[0], dims, preferred_element_type=F32)
            at = slice(3 * TAPS, 3 * TAPS + sz.ch)

        @pl.when(member == 0)
        def _():
            acc[:, at] = term + acc_in[:, at] if chunk else term

        @pl.when(member > 0)
        def _():
            acc[:, at] = acc[:, at] + term

    for side in range(2):
        if (side == 0 and chunk == 0) or (side == 1 and final):
            col = 0 if side == 0 else sz.cpos - width
            part = jnp.dot(
                wt3[0 if side == 0 else 2], gpre[:, col : col + width], preferred_element_type=F32
            )
            edge_out[0, side if sz.chunks == 1 else 0] = fold_taps(part, sz.ch)

    @pl.when(member == sz.mem - 1)
    def _():
        used = 3 * TAPS + sz.ch
        wg_out[:, :used] = acc[...].astype(wg_out.dtype)
        if final:
            wg_out[:, used:] = jnp.zeros((sz.hid, wg_out.shape[1] - used), wg_out.dtype)


def data_kernel(sz, *refs):
    gpres, gps = refs[: sz.chunks], refs[sz.chunks : 2 * sz.chunks]
    wt3, from_dn, from_up, out, gs = refs[2 * sz.chunks :]
    width = sz.lon

    def two_rows(first):
        cols = []
        for row in (first, first + 1):
            if row < 0 or row >= sz.lat:
                cols.append(jnp.zeros((sz.hid, width), BF16))
            else:
                at = row % sz.crows * width
                cols.append(gpres[row // sz.crows][0, :, at : at + width])
        return jnp.concatenate(cols, axis=1)

    for pair in range(sz.lat // 2):
        part = None
        for ro in range(3):
            term = jnp.dot(wt3[ro], two_rows(pair * 2 + 1 - ro), preferred_element_type=F32)
            part = term if part is None else part + term
        for i in range(2):
            row = pair * 2 + i
            at = row % sz.crows * width
            total = gps[row // sz.crows][0, :, at : at + width].astype(F32) + fold_taps(
                part[:, i * width : (i + 1) * width], sz.ch
            )
            if row == 0:
                total = total + from_up[0, 0]
            if row == sz.lat - 1:
                total = total + from_dn[0, 0]
            gs[pl.ds(row, sz.ch, stride=sz.lat), :] = total
    out[0] = gs[...].reshape(sz.ch, sz.lat, width).astype(BF16)


def whole(shape):
    return pl.BlockSpec(shape, lambda *_: (0,) * len(shape))


def by_member(*shape):
    return pl.BlockSpec((1,) + shape, lambda m, *_: (m,) + (0,) * len(shape))


def array(shape, dtype):
    return jax.ShapeDtypeStruct(shape, dtype)


def cost(flops, moved, transcendentals=0):
    return pl.CostEstimate(flops=flops, bytes_accessed=moved, transcendentals=transcendentals)


def on_device(states, noise_field, target, w_conv, w_proj, matchings):
    member_count = lax.axis_size("member")
    band_count = lax.axis_size("band")
    sz = Sizes(states, w_conv, member_count)
    mem, ch, lat, lon, hid, pos = sz.mem, sz.ch, sz.lat, sz.lon, sz.hid, sz.pos
    cpos, chunks = sz.cpos, sz.chunks
    count = matchings.shape[0]
    members = mem * member_count
    down = [(i, i + 1) for i in range(band_count - 1)]
    up = [(i + 1, i) for i in range(band_count - 1)]

    def edge(row):
        return (
            states[:, :, row : row + 1].astype(F32) + noise_field[:, :, row : row + 1]
        ).astype(BF16)

    halo_up = lax.ppermute(edge(lat - 1), "band", down)
    halo_dn = lax.ppermute(edge(0), "band", up)

    e_in, x_in, truth, w3 = pl.pallas_call(
        functools.partial(prep_kernel, sz),
        grid=(mem,),
        in_specs=[
            by_member(ch, lat, lon),
            by_member(ch, lat, lon),
            whole((ch, lat, lon)),
            whole(w_conv.shape),
        ],
        out_specs=[
            by_member(TAPS, pos),
            by_member(ch, pos),
            whole((chunks, sz.devs, ch, LANES)),
            whole((hid, 3 * TAPS)),
        ],
        out_shape=[
            array((mem, TAPS, pos), BF16),
            array((mem, ch, pos), BF16),
            array((chunks, sz.devs, ch, LANES), BF16),
            array((hid, 3 * TAPS), BF16),
        ],
        scratch_shapes=[pltpu.VMEM((ch * lat, lon), F32), pltpu.VMEM((TAPS, lon), F32)],
        compiler_params=vmem_params(1),
        cost_estimate=cost(10_000_000, 8_000_000),
        name="prep",
    )(states, noise_field, target, w_conv)

    half_proj = w_proj * jnp.asarray(0.5, BF16)
    conv_flops = 2 * mem * cpos * hid * 3 * TAPS
    hidden, slope, snd = [], [], []
    for chunk in range(chunks):
        outs = pl.pallas_call(
            functools.partial(forward_kernel, sz, chunk),
            grid=(mem,),
            in_specs=[
                by_member(TAPS, pos),
                pl.BlockSpec((1, ch, cpos), lambda m, chunk=chunk: (m, 0, chunk)),
                by_member(ch, 1, lon),
                by_member(ch, 1, lon),
                whole((hid, 3 * TAPS)),
                whole(w_proj.shape),
            ],
            out_specs=[
                by_member(hid, cpos),
                by_member(hid, cpos),
                whole((sz.devs, sz.sub, LANES)),
            ],
            out_shape=[
                array((mem, hid, cpos), BF16),
                array((mem, hid, cpos), BF16),
                array((sz.devs, sz.sub, LANES), BF16),
            ],
            scratch_shapes=[
                pltpu.VMEM((TAPS, cpos + 2 * lon), BF16),
                pltpu.VMEM((TAPS, lon), F32),
                pltpu.VMEM((sz.devs, sz.sub, LANES), F32),
            ],
            compiler_params=vmem_params(1),
            cost_estimate=cost(conv_flops, 9_000_000, 2 * mem * cpos * hid),
            name=f"forward{chunk}",
        )(e_in, x_in, halo_up, halo_dn, w3, half_proj)
        hidden.append(outs[0])
        slope.append(outs[1])
        snd.append(outs[2])

    device = lax.axis_index("member").astype(jnp.int32).reshape(1)
    rows = (count + 1) * members
    preds = [lax.all_to_all(part, "member", 0, 0, tiled=True) for part in snd]
    back = []
    for chunk in range(chunks):
        grads = pl.pallas_call(
            functools.partial(pair_kernel, sz, count),
            grid_spec=pltpu.PrefetchScalarGridSpec(
                num_scalar_prefetch=2,
                grid=(1,),
                in_specs=[
                    whole((sz.devs, sz.sub, LANES)),
                    pl.BlockSpec(
                        (1, 1, ch, LANES),
                        lambda i, match, device, chunk=chunk: (chunk, device[0], 0, 0),
                    ),
                ],
                out_specs=whole((sz.devs, sz.sub, LANES)),
                scratch_shapes=[
                    pltpu.VMEM((members, sz.chpad, LANES), F32),
                    pltpu.VMEM((sz.chpad, LANES), F32),
                    pltpu.VMEM((rows * 8, LANES), F32),
                    pltpu.VMEM((rows, LANES), F32),
                    pltpu.VMEM((sz.sub, LANES), F32),
                    pltpu.SMEM((count, members), jnp.int32),
                ],
            ),
            out_shape=array((sz.devs, sz.sub, LANES), BF16),
            compiler_params=vmem_params(1),
            cost_estimate=cost(members * 20 * sz.chpad * LANES, 2_000_000),
            name=f"pairs{chunk}",
        )(matchings, device, preds[chunk], truth)
        back.append(lax.all_to_all(grads, "member", 0, 0, tiled=True))

    late_conv, late_proj, _ = lax.optimization_barrier((w_conv, half_proj, snd[0]))
    w_proj_t = late_proj.T
    wt3 = jnp.pad(late_conv.T.reshape(3, 3 * ch, hid), ((0, 0), (0, TAPS - 3 * ch), (0, 0)))
    used = 3 * TAPS + ch
    cols = (used + LANES - 1) // LANES * LANES
    grad_pred, grad_pre, edges = [], [], []
    partial = None
    for chunk in range(chunks):
        final = chunk == chunks - 1
        wg_shape = (hid, cols) if final else (hid, used)
        sides = 2 if chunks == 1 else 1
        extra = [] if partial is None else [partial]
        outs = pl.pallas_call(
            functools.partial(weight_kernel, sz, chunk),
            grid=(mem,),
            in_specs=[
                whole((sz.devs, sz.sub, LANES)),
                by_member(hid, cpos),
                by_member(hid, cpos),
                by_member(TAPS, pos),
                by_member(ch, 1, lon),
                by_member(ch, 1, lon),
                whole(w_proj_t.shape),
                whole(wt3.shape),
            ]
            + [whole((hid, used)) for _ in extra],
            out_specs=[
                by_member(ch, cpos),
                by_member(hid, cpos),
                whole(wg_shape),
                by_member(sides, ch, lon),
            ],
            out_shape=[
                array((mem, ch, cpos), BF16),
                array((mem, hid, cpos), BF16),
                array(wg_shape, BF16 if final else F32),
                array((mem, sides, ch, lon), F32),
            ],
            scratch_shapes=[
                pltpu.VMEM((TAPS, cpos + 2 * lon), BF16),
                pltpu.VMEM((TAPS, lon), F32),
                pltpu.VMEM((8, sz.sub, LANES), F32),
                pltpu.VMEM((hid, used), F32),
            ],
            compiler_params=vmem_params(1),
            cost_estimate=cost(conv_flops, 9_000_000),
            name=f"weights{chunk}",
        )(back[chunk], hidden[chunk], slope[chunk], e_in, halo_up, halo_dn, w_proj_t, wt3, *extra)
        grad_pred.append(outs[0])
        grad_pre.append(outs[1])
        partial = outs[2]
        edges.append(outs[3])

    shards = member_count * band_count
    terms = lax.all_to_all(
        partial.reshape(shards, hid // shards, cols), ("member", "band"), 0, 0, tiled=True
    )
    from_dn = lax.ppermute(edges[0][:, 0:1], "band", up)
    from_up = lax.ppermute(edges[-1][:, -1:], "band", down)

    grad_states = pl.pallas_call(
        functools.partial(data_kernel, sz),
        grid=(mem,),
        in_specs=[by_member(hid, cpos)] * chunks
        + [by_member(ch, cpos)] * chunks
        + [whole(wt3.shape), by_member(1, ch, lon), by_member(1, ch, lon)],
        out_specs=by_member(ch, lat, lon),
        out_shape=array((mem, ch, lat, lon), BF16),
        scratch_shapes=[pltpu.VMEM((ch * lat, lon), F32)],
        compiler_params=vmem_params(1),
        cost_estimate=cost(chunks * conv_flops, 8_000_000),
        name="data",
    )(*grad_pre, *grad_pred, wt3, from_dn, from_up)

    factor = 1.0 / (pos * members * band_count) ** 0.5
    total = jnp.sum(terms.astype(F32), axis=0)
    own = hid // shards
    grad_conv = total[:, : 3 * TAPS].reshape(own, 3, TAPS)[:, :, : 3 * ch].reshape(own, 9 * ch)
    grad_proj = total[:, 3 * TAPS : 3 * TAPS + ch].T
    return grad_states, grad_conv * factor, grad_proj * (0.5 * factor)


def solution(mesh):
    return jax.shard_map(
        on_device,
        mesh=mesh,
        in_specs=(
            P("member", None, "band", None),
            P("member", None, "band", None),
            P(None, "band", None),
            P(),
            P(),
            P(),
        ),
        out_specs=(
            P("member", None, "band", None),
            P(("member", "band"), None),
            P(None, ("member", "band")),
        ),
        check_vma=False,
    )
```

```python
import functools

import jax
import jax.numpy as jnp
from jax import lax
from jax.experimental import pallas as pl
from jax.experimental.pallas import tpu as pltpu
from jax.sharding import PartitionSpec as P

SQRT_HALF = 0.7071067811865476
INV_ROOT_TWO_PI = 0.3989422804014327
F32 = jnp.float32
BF16 = jnp.bfloat16
LANES = 128
TAPS = 256
LOG2_E = 1.4426950408889634


def call(kernel, name, outs, scratch, flops, moved, args, smem=(), limit=24, aliases=None):
    vmem = pl.BlockSpec(memory_space=pltpu.VMEM)
    scalars = pl.BlockSpec(memory_space=pltpu.SMEM)
    return pl.pallas_call(
        kernel,
        in_specs=[scalars if i in smem else vmem for i in range(len(args))],
        out_specs=[vmem] * len(outs),
        out_shape=[jax.ShapeDtypeStruct(*out) for out in outs],
        scratch_shapes=scratch,
        input_output_aliases=aliases or {},
        compiler_params=pltpu.CompilerParams(vmem_limit_bytes=limit * 1024 * 1024),
        cost_estimate=pl.CostEstimate(flops=flops, bytes_accessed=moved, transcendentals=0),
        name=name,
    )(*args)


def shift_right(vals):
    lane = lax.broadcasted_iota(jnp.int32, vals.shape, 1)
    return jnp.where(lane == 0, 0.0, pltpu.roll(vals, 1, 1))


def shift_left(vals):
    width = vals.shape[1]
    lane = lax.broadcasted_iota(jnp.int32, vals.shape, 1)
    return jnp.where(lane == width - 1, 0.0, pltpu.roll(vals, width - 1, 1))


def expand_row(vals, scratch):
    channels = vals.shape[0]
    scratch[pl.ds(0, channels), :] = shift_right(vals)
    scratch[pl.ds(channels, channels), :] = vals
    scratch[pl.ds(2 * channels, channels), :] = shift_left(vals)
    return scratch[...].astype(BF16)


def swap_blocks(rows):
    parts = len(rows)
    size = rows[0].shape[1] // parts
    lane = lax.broadcasted_iota(jnp.int32, rows[0].shape, 1)
    rows = list(rows)
    bit = 1
    while bit < parts:
        low = (lane & (bit * size)) == 0
        shift = bit * size
        width = rows[0].shape[1]
        for i in range(parts):
            if i & bit:
                continue
            a, b = rows[i], rows[i | bit]
            rows[i] = jnp.where(low, a, pltpu.roll(b, shift, 1))
            rows[i | bit] = jnp.where(low, pltpu.roll(a, width - shift, 1), b)
        bit *= 2
    return rows


class Sizes:
    def __init__(self, states, w_conv, member_count, band_count):
        self.mem, self.ch, self.lat, self.lon = states.shape
        self.hid = w_conv.shape[0]
        self.devs = member_count
        self.bands = band_count
        self.members = self.mem * member_count
        self.prows = self.lat // 8
        self.parts = member_count // self.prows
        self.groups = 8 // self.parts
        self.sub = self.groups * self.ch
        self.subpad = (self.sub + 7) // 8 * 8
        self.pos = self.lat * self.lon
        self.used = 3 * TAPS + self.ch
        self.cols = (self.used + LANES - 1) // LANES * LANES


def prep_kernel(sz, states, noise, target, wt3, e_out, x_out, t_out, w_out, xs, es, ps):
    es[...] = jnp.zeros_like(es)

    def one(m, carry):
        x = (states[m].astype(F32) + noise[m]).astype(BF16)
        xs[...] = x.astype(F32).reshape(sz.ch * sz.lat, sz.lon)
        for row in range(sz.lat):
            vals = xs[pl.ds(row, sz.ch, stride=sz.lat), :]
            x_out[m, :, row * sz.lon : (row + 1) * sz.lon] = vals.astype(BF16)
            e_out[m, :, (row + 1) * sz.lon : (row + 2) * sz.lon] = expand_row(vals, es)
        return carry

    lax.fori_loop(0, sz.mem, one, 0)
    xs[...] = target[...].astype(F32).reshape(sz.ch * sz.lat, sz.lon)
    if sz.subpad > sz.sub:
        ps[...] = jnp.zeros_like(ps)
    for prow in range(sz.prows):
        for group in range(sz.groups):
            first = prow * 8 + group * sz.parts
            rows = [xs[pl.ds(first + i, sz.ch, stride=sz.lat), :] for i in range(sz.parts)]
            for q, out in enumerate(swap_blocks(rows)):
                ps[q, pl.ds(group * sz.ch, sz.ch), :] = out
        for q in range(sz.parts):
            t_out[prow * sz.parts + q] = ps[q].astype(BF16)
    for ro in range(3):
        w_out[:, ro * TAPS : (ro + 1) * TAPS] = wt3[ro].T


def halo_row(sz, halos, band, side, m):
    other = band - 1 if side == 0 else band + 1
    inside = jnp.logical_and(other >= 0, other < sz.bands)
    vals = halos[jnp.clip(other, 0, sz.bands - 1), m].astype(F32)
    return vals * jnp.where(inside, 1.0, 0.0)


def forward_kernel(sz, place, e_in, x_in, halos, w3, w_proj, pre_out, hid_out, ext, snd, es, ps, preds):
    width = sz.lon
    pairs = sz.lat // 2
    es[...] = jnp.zeros_like(es)
    if sz.subpad > sz.sub:
        ps[...] = jnp.zeros_like(ps)

    def one(m, carry):
        ext[m, :, width : width + sz.pos] = e_in[m, :, width : width + sz.pos]
        for side in range(2):
            at = 0 if side == 0 else width + sz.pos
            ext[m, :, at : at + width] = expand_row(halo_row(sz, halos, place[1], side, m), es)

        def conv(pair):
            cols = jnp.concatenate(
                [ext[m, :, (pair * 2 + ro) * width : (pair * 2 + ro + 2) * width] for ro in range(3)],
                axis=0,
            )
            pre_out[m, :, pair * 2 * width : (pair + 1) * 2 * width] = jnp.dot(
                w3[...], cols, preferred_element_type=F32
            )

        def rest(pair):
            here = slice(pair * 2 * width, (pair + 1) * 2 * width)
            preact = pre_out[m, :, here]
            hidden = (preact * (1.0 + lax.erf(preact * SQRT_HALF))).astype(BF16)
            hid_out[m, :, here] = hidden
            pred = x_in[m, :, here].astype(F32) + 0.5 * jnp.dot(
                w_proj[...], hidden, preferred_element_type=F32
            )
            preds[:, here] = pred.astype(BF16).astype(F32)

        conv(0)
        for pair in range(pairs):
            if pair + 1 < pairs:
                conv(pair + 1)
            rest(pair)
        for prow in range(sz.prows):
            for group in range(sz.groups):
                first = prow * 8 + group * sz.parts
                rows = [
                    preds[:, (first + i) * width : (first + i + 1) * width]
                    for i in range(sz.parts)
                ]
                for q, out in enumerate(swap_blocks(rows)):
                    ps[q, pl.ds(group * sz.ch, sz.ch), :] = out
            for q in range(sz.parts):
                snd[prow * sz.parts + q, m] = ps[q].astype(BF16)
        return carry

    lax.fori_loop(0, sz.mem, one, 0)


def slope_kernel(sz, preact, slope):
    rows = 32
    per = sz.hid // rows

    def one(i, carry):
        m = i // per
        at = pl.ds(pl.multiple_of(i % per * rows, rows), rows)
        x = preact[m, at, :]
        twice = 1.0 + lax.erf(x * SQRT_HALF)
        bell = jnp.exp2(x * x * (-0.5 * LOG2_E)) * (2.0 * INV_ROOT_TWO_PI)
        slope[m, at, :] = twice + x * bell
        return carry

    lax.fori_loop(0, sz.mem * per, one, 0)


def pair_kernel(sz, count, match, place, preds, truth, grads, vals, tsc, sums, scale, inv):
    norm = 1.0 / (32.0 * sz.ch)
    members = sz.members
    folds = sz.subpad // 8
    vals[...] = preds[...].reshape(members, sz.subpad, LANES).astype(F32)
    tsc[...] = truth[place[0]].astype(F32)

    def squares(diff):
        return jnp.sum((diff * diff).reshape(folds, 8, LANES), axis=0)

    def first(m, carry):
        own = vals[m]
        sums[pl.ds(pl.multiple_of((count * members + m) * 8, 8), 8), :] = squares(own - tsc[...])
        for k in range(count):
            other = match[k, m]
            inv[k, other] = m
            at = pl.multiple_of((k * members + m) * 8, 8)
            sums[pl.ds(at, 8), :] = squares(own - vals[other])
        return carry

    lax.fori_loop(0, members, first, 0)
    rows = (count + 1) * members
    total = sums[pl.ds(0, rows, stride=8), :]
    for j in range(1, 8):
        total = total + sums[pl.ds(j, rows, stride=8), :]
    step = sz.lon // sz.parts
    while step < LANES:
        total = total + pltpu.roll(total, step, 1)
        step *= 2
    lane = lax.broadcasted_iota(jnp.int32, total.shape, 1)
    for bit in (1, 2):
        total = total + jnp.where(
            (lane & bit) == 0, pltpu.roll(total, LANES - bit, 1), pltpu.roll(total, bit, 1)
        )
    inverse = lax.rsqrt(total * norm + 1e-06)
    scale[pl.ds(0, count * members), :] = inverse[: count * members] * (0.5 / count)
    scale[pl.ds(count * members, members), :] = inverse[count * members :]

    def second(m, carry):
        weight = scale[pl.ds(count * members + m, 1), :]
        acc = None
        own_weight = weight
        for k in range(count):
            back = inv[k, m]
            for other, index in ((match[k, m], k * members + m), (back, k * members + back)):
                part = scale[pl.ds(index, 1), :]
                own_weight = own_weight - part
                term = part * vals[other]
                acc = term if acc is None else acc + term
        out = own_weight * vals[m] + (acc - weight * tsc[...])
        grads[m // sz.mem, m % sz.mem] = out.astype(BF16)
        return carry

    lax.fori_loop(0, members, second, 0)


def fold_taps(part, channels):
    return (
        part[channels : 2 * channels]
        + shift_left(part[0:channels])
        + shift_right(part[2 * channels : 3 * channels])
    )


def weight_sums(sz, core, gpre, hid, ext, gp, store):
    block = sz.hid // sz.devs

    def take(ref):
        rows = []
        for z in range(sz.devs // 2):
            at = pl.ds(pl.multiple_of((2 * z + core) * block, block), block)
            rows.append(jnp.concatenate([ref[m, at, :] for m in range(sz.mem)], axis=1))
        return jnp.concatenate(rows, axis=0)

    dims = (((1,), (1,)), ((), ()))
    left = take(gpre)
    for ro in range(3):
        cols = [ext[m, :, ro * sz.lon : ro * sz.lon + sz.pos] for m in range(sz.mem)]
        store(
            ro * TAPS,
            lax.dot_general(
                left, jnp.concatenate(cols, axis=1), dims, preferred_element_type=F32
            ),
        )
    cols = [gp[m] for m in range(sz.mem)]
    store(
        3 * TAPS,
        0.5
        * lax.dot_general(
            take(hid), jnp.concatenate(cols, axis=1), dims, preferred_element_type=F32
        ),
    )
    store(sz.used, jnp.zeros((sz.hid // 2, sz.cols - sz.used), F32))


def sibling_kernel(sz, place, back, slope, hid, ext, w_proj, wt3, gp, gpre, edges, sib, rows_f, wpt):
    width = sz.lon
    wpt[...] = (w_proj[...].astype(F32) * 0.5).T.astype(BF16)

    def one(m, carry):
        for prow in range(sz.prows):
            for q in range(sz.parts):
                rows_f[q] = back[prow * sz.parts + q, m].astype(F32)
            for group in range(sz.groups):
                outs = swap_blocks(
                    [rows_f[q, pl.ds(group * sz.ch, sz.ch), :] for q in range(sz.parts)]
                )
                for i, out in enumerate(outs):
                    row = prow * 8 + group * sz.parts + i
                    gp[m, :, row * width : (row + 1) * width] = out.astype(BF16)
        for pair in range(sz.lat // 2):
            here = slice(pair * 2 * width, (pair + 1) * 2 * width)
            dhid = jnp.dot(wpt[...], gp[m, :, here], preferred_element_type=F32)
            gpre[m, :, here] = (dhid * slope[m, :, here]).astype(BF16)
        for side in range(2):
            at = 0 if side == 0 else sz.pos - width
            part = jnp.dot(
                wt3[2 * side], gpre[m, :, at : at + width], preferred_element_type=F32
            )
            edges[side, m] = fold_taps(part, sz.ch)
        return carry

    lax.fori_loop(0, sz.mem, one, 0)

    def store(at, term):
        sib[:, at : at + term.shape[1]] = term.astype(BF16)

    weight_sums(sz, 1 - place[2], gpre, hid, ext, gp, store)


def own_kernel(sz, place, gpre, hid, ext, gp, own):
    def store(at, term):
        own[:, at : at + term.shape[1]] = term

    weight_sums(sz, place[2], gpre, hid, ext, gp, store)


def data_kernel(sz, gpre, gp, wt3, from_dn, from_up, out, gs):
    width = sz.lon

    def one(m, carry):
        def two_rows(first):
            low, high = max(first, 0), min(first + 2, sz.lat)
            cols = [gpre[m, :, low * width : high * width]]
            zero = jnp.zeros((sz.hid, width), BF16)
            if first < 0:
                cols.insert(0, zero)
            if first + 2 > sz.lat:
                cols.append(zero)
            return cols[0] if len(cols) == 1 else jnp.concatenate(cols, axis=1)

        for pair in range(sz.lat // 2):
            part = None
            for ro in range(3):
                term = jnp.dot(wt3[ro], two_rows(pair * 2 + 1 - ro), preferred_element_type=F32)
                part = term if part is None else part + term
            for i in range(2):
                row = pair * 2 + i
                at = row * width
                total = gp[m, :, at : at + width].astype(F32) + fold_taps(
                    part[:, i * width : (i + 1) * width], sz.ch
                )
                if row == 0:
                    total = total + from_up[m]
                if row == sz.lat - 1:
                    total = total + from_dn[m]
                gs[pl.ds(row, sz.ch, stride=sz.lat), :] = total
        out[m] = gs[...].reshape(sz.ch, sz.lat, width).astype(BF16)
        return carry

    lax.fori_loop(0, sz.mem, one, 0)


MEMBER = ("pair", "core")


def on_device(states, noise_field, target, w_conv, w_proj, matchings):
    member_count = lax.axis_size("pair") * lax.axis_size("core")
    band_count = lax.axis_size("band")
    sz = Sizes(states, w_conv, member_count, band_count)
    mem, ch, lat, lon, hid, pos = sz.mem, sz.ch, sz.lat, sz.lon, sz.hid, sz.pos
    count = matchings.shape[0]
    down = [(i, i + 1) for i in range(band_count - 1)]
    up = [(i + 1, i) for i in range(band_count - 1)]
    band = lax.axis_index("band").astype(jnp.int32)
    core = lax.axis_index("core").astype(jnp.int32)
    member = lax.axis_index("pair").astype(jnp.int32) * lax.axis_size("core") + core
    place = jnp.stack([member, band, core])

    def edge(row):
        return (states[:, :, row].astype(F32) + noise_field[:, :, row]).astype(BF16)

    after = (jnp.arange(band_count, dtype=jnp.int32) > band)[:, None, None, None]
    halos = lax.all_to_all(
        jnp.where(after, edge(lat - 1)[None], edge(0)[None]), "band", 0, 0, tiled=True
    )
    wt3 = jnp.pad(w_conv.T.reshape(3, 3 * ch, hid), ((0, 0), (0, TAPS - 3 * ch), (0, 0)))

    ext_shape = (mem, TAPS, pos + 2 * lon)
    e_in, x_in, truth, w3 = call(
        functools.partial(prep_kernel, sz),
        "prep",
        [
            (ext_shape, BF16),
            ((mem, ch, pos), BF16),
            ((sz.devs, sz.subpad, LANES), BF16),
            ((hid, 3 * TAPS), BF16),
        ],
        [
            pltpu.VMEM((ch * lat, lon), F32),
            pltpu.VMEM((TAPS, lon), F32),
            pltpu.VMEM((sz.parts, sz.subpad, LANES), F32),
        ],
        10_000_000,
        8_000_000,
        (states, noise_field, target, wt3),
    )

    conv_flops = 2 * mem * pos * hid * 3 * TAPS
    preact, hidden, ext, snd = call(
        functools.partial(forward_kernel, sz),
        "forward",
        [
            ((mem, hid, pos), F32),
            ((mem, hid, pos), BF16),
            (ext_shape, BF16),
            ((sz.devs, mem, sz.subpad, LANES), BF16),
        ],
        [
            pltpu.VMEM((TAPS, lon), F32),
            pltpu.VMEM((sz.parts, sz.subpad, LANES), F32),
            pltpu.VMEM((ch, pos), F32),
        ],
        conv_flops,
        9_000_000,
        (place, e_in, x_in, halos, w3, w_proj),
        smem=(0,),
        aliases={1: 2},
    )

    preds = lax.all_to_all(snd, MEMBER, 0, 0, tiled=True)
    preact, _ = lax.optimization_barrier((preact, snd))
    (slope,) = call(
        functools.partial(slope_kernel, sz),
        "slope",
        [((mem, hid, pos), F32)],
        [],
        10 * mem * hid * pos,
        8 * mem * hid * pos,
        (preact,),
        aliases={0: 0},
    )

    rows = (count + 1) * sz.members
    (grads,) = call(
        functools.partial(pair_kernel, sz, count),
        "pairs",
        [((sz.devs, mem, sz.subpad, LANES), BF16)],
        [
            pltpu.VMEM((sz.members, sz.subpad, LANES), F32),
            pltpu.VMEM((sz.subpad, LANES), F32),
            pltpu.VMEM((rows * 8, LANES), F32),
            pltpu.VMEM((rows, LANES), F32),
            pltpu.SMEM((count, sz.members), jnp.int32),
        ],
        sz.members * 30 * sz.subpad * LANES,
        2_000_000,
        (matchings, place, preds, truth),
        smem=(0, 1),
    )
    back = lax.all_to_all(grads, MEMBER, 0, 0, tiled=True)

    half = (hid // 2, sz.cols)
    grad_pred, grad_pre, edges, sibling = call(
        functools.partial(sibling_kernel, sz),
        "sibling",
        [
            ((mem, ch, pos), BF16),
            ((mem, hid, pos), BF16),
            ((2, mem, ch, lon), F32),
            (half, BF16),
        ],
        [pltpu.VMEM((sz.parts, sz.subpad, LANES), F32), pltpu.VMEM((hid, ch), BF16)],
        conv_flops,
        9_000_000,
        (place, back, slope, hidden, ext, w_proj, wt3),
        smem=(0,),
    )
    swapped = lax.ppermute(sibling, "core", [(0, 1), (1, 0)])
    (own,) = call(
        functools.partial(own_kernel, sz),
        "own",
        [(half, F32)],
        [],
        conv_flops // 2,
        9_000_000,
        (place, grad_pre, hidden, ext, grad_pred),
        smem=(0,),
    )
    shards = member_count * band_count
    each = hid // shards
    partial = (own + swapped.astype(F32)).astype(BF16).reshape(shards // 2, each, sz.cols)
    terms = lax.all_to_all(partial, ("pair", "band"), 0, 0, tiled=True)
    edges, _ = lax.optimization_barrier((edges, own))
    from_dn = lax.ppermute(edges[0], "band", up)
    from_up = lax.ppermute(edges[1], "band", down)

    (grad_states,) = call(
        functools.partial(data_kernel, sz),
        "data",
        [((mem, ch, lat, lon), BF16)],
        [pltpu.VMEM((ch * lat, lon), F32)],
        conv_flops,
        8_000_000,
        (grad_pre, grad_pred, wt3, from_dn, from_up),
    )

    factor = 1.0 / (pos * sz.members * band_count) ** 0.5
    total = jnp.sum(terms.astype(F32), axis=0) * factor
    grad_conv = total[:, : 3 * TAPS].reshape(each, 3, TAPS)[:, :, : 3 * ch].reshape(each, 9 * ch)
    grad_proj = total[:, 3 * TAPS : sz.used].T
    return grad_states, grad_conv, grad_proj


def solution(mesh):
    members = mesh.shape["member"]
    split = jax.sharding.Mesh(
        mesh.devices.reshape(members // 2, 2, mesh.shape["band"]), MEMBER + ("band",)
    )
    return jax.shard_map(
        on_device,
        mesh=split,
        in_specs=(
            P(MEMBER, None, "band", None),
            P(MEMBER, None, "band", None),
            P(None, "band", None),
            P(),
            P(),
            P(),
        ),
        out_specs=(
            P(MEMBER, None, "band", None),
            P(MEMBER + ("band",), None),
            P(None, MEMBER + ("band",)),
        ),
        check_vma=False,
    )
```

```python
import functools

import jax
import jax.numpy as jnp
from jax import lax
from jax.experimental import pallas as pl
from jax.experimental.pallas import tpu as pltpu
from jax.sharding import PartitionSpec as P

SQRT_HALF = 0.7071067811865476
INV_ROOT_TWO_PI = 0.3989422804014327
F32 = jnp.float32
BF16 = jnp.bfloat16
LANES = 128
TAPS = 256
LOG2_E = 1.4426950408889634


def call(kernel, name, outs, scratch, flops, moved, args, smem=(), vmem=(), vmem_outs=(), limit=60):
    kinds = {"hbm": pltpu.HBM, "vmem": pltpu.VMEM, "smem": pltpu.SMEM}
    specs = {kind: pl.BlockSpec(memory_space=space) for kind, space in kinds.items()}

    def kind(i):
        return "smem" if i in smem else "vmem" if i in vmem else "hbm"

    return pl.pallas_call(
        kernel,
        in_specs=[specs[kind(i)] for i in range(len(args))],
        out_specs=[specs["vmem" if i in vmem_outs else "hbm"] for i in range(len(outs))],
        out_shape=[jax.ShapeDtypeStruct(*out) for out in outs],
        scratch_shapes=scratch,
        compiler_params=pltpu.CompilerParams(vmem_limit_bytes=limit * 1024 * 1024),
        cost_estimate=pl.CostEstimate(flops=flops, bytes_accessed=moved, transcendentals=0),
        name=name,
    )(*args)


class Copies:
    def __init__(self, sems):
        self.sems, self.used, self.open = sems, 0, []

    def start(self, src, dst):
        copy = pltpu.make_async_copy(src, dst, self.sems.at[self.used])
        self.used += 1
        copy.start()
        self.open.append(copy)
        return copy

    def finish(self, copies=None):
        for copy in list(self.open) if copies is None else copies:
            if any(copy is other for other in self.open):
                self.open = [other for other in self.open if other is not copy]
                copy.wait()


def dma(count):
    return pltpu.SemaphoreType.DMA((count,))


def shift_right(vals):
    lane = lax.broadcasted_iota(jnp.int32, vals.shape, 1)
    return jnp.where(lane == 0, 0.0, pltpu.roll(vals, 1, 1))


def shift_left(vals):
    width = vals.shape[1]
    lane = lax.broadcasted_iota(jnp.int32, vals.shape, 1)
    return jnp.where(lane == width - 1, 0.0, pltpu.roll(vals, width - 1, 1))


def expand_row(vals, scratch):
    channels = vals.shape[0]
    scratch[pl.ds(0, channels), :] = shift_right(vals)
    scratch[pl.ds(channels, channels), :] = vals
    scratch[pl.ds(2 * channels, channels), :] = shift_left(vals)
    return scratch[...].astype(BF16)


def swap_blocks(rows):
    parts = len(rows)
    size = rows[0].shape[1] // parts
    lane = lax.broadcasted_iota(jnp.int32, rows[0].shape, 1)
    rows = list(rows)
    bit = 1
    while bit < parts:
        low = (lane & (bit * size)) == 0
        shift = bit * size
        width = rows[0].shape[1]
        for i in range(parts):
            if i & bit:
                continue
            a, b = rows[i], rows[i | bit]
            rows[i] = jnp.where(low, a, pltpu.roll(b, shift, 1))
            rows[i | bit] = jnp.where(low, pltpu.roll(a, width - shift, 1), b)
        bit *= 2
    return rows


class Sizes:
    def __init__(self, states, w_conv, member_count, band_count):
        self.mem, self.ch, self.lat, self.lon = states.shape
        self.hid = w_conv.shape[0]
        self.devs = member_count
        self.bands = band_count
        self.members = self.mem * member_count
        self.prows = self.lat // 8
        self.parts = member_count // self.prows
        self.groups = 8 // self.parts
        self.sub = self.groups * self.ch
        self.subpad = (self.sub + 7) // 8 * 8
        self.pos = self.lat * self.lon
        self.used = 3 * TAPS + self.ch
        self.cols = (self.used + LANES - 1) // LANES * LANES


def inputs_kernel(sz, place, states, noise, x_out, send, st, ns, xs, xv, sv, rows, sems):
    copies = Copies(sems)
    loads = []
    for m in range(sz.mem):
        loads.append(
            [copies.start(states.at[m], st.at[m]), copies.start(noise.at[m], ns.at[m])]
        )
    for m in range(sz.mem):
        copies.finish(loads[m])
        xs[...] = (st[m].astype(F32) + ns[m]).astype(BF16).astype(F32).reshape(
            sz.ch * sz.lat, sz.lon
        )
        for row in range(sz.lat):
            vals = xs[pl.ds(row, sz.ch, stride=sz.lat), :].astype(BF16)
            xv[m, :, row * sz.lon : (row + 1) * sz.lon] = vals
        first = xs[pl.ds(0, sz.ch, stride=sz.lat), :]
        last = xs[pl.ds(sz.lat - 1, sz.ch, stride=sz.lat), :]
        rows[0, pl.ds(m * sz.ch, sz.ch), :] = first
        rows[1, pl.ds(m * sz.ch, sz.ch), :] = last
        copies.start(xv.at[m], x_out.at[m])
    for other in range(sz.bands):
        after = jnp.where(other > place[1], 1.0, 0.0)
        sv[other] = (rows[1] * after + rows[0] * (1.0 - after)).astype(BF16)
    copies.start(sv, send)
    copies.finish()


def prep_kernel(sz, x_in, target, wt3, e_out, t_out, w_out, xv, tv, wv, ev, tov, wov, xs, es, ps, sems):
    copies = Copies(sems)
    x_loads = [copies.start(x_in.at[m], xv.at[m]) for m in range(sz.mem)]
    t_load = copies.start(target, tv)
    w_load = copies.start(wt3, wv)
    es[...] = jnp.zeros_like(es)
    inner = slice(sz.lon, sz.lon + sz.pos)
    for m in range(sz.mem):
        copies.finish([x_loads[m]])
        for row in range(sz.lat):
            here = slice(row * sz.lon, (row + 1) * sz.lon)
            ev[m, :, here] = expand_row(xv[m, :, here].astype(F32), es)
        copies.start(ev.at[m], e_out.at[m, :, inner])
    copies.finish([t_load])
    xs[...] = tv[...].astype(F32).reshape(sz.ch * sz.lat, sz.lon)
    if sz.subpad > sz.sub:
        ps[...] = jnp.zeros_like(ps)
    for prow in range(sz.prows):
        for group in range(sz.groups):
            first = prow * 8 + group * sz.parts
            rows = [xs[pl.ds(first + i, sz.ch, stride=sz.lat), :] for i in range(sz.parts)]
            for q, out in enumerate(swap_blocks(rows)):
                ps[q, pl.ds(group * sz.ch, sz.ch), :] = out
        for q in range(sz.parts):
            tov[prow * sz.parts + q] = ps[q].astype(BF16)
    copies.start(tov, t_out)
    copies.finish([w_load])
    for ro in range(3):
        wov[:, ro * TAPS : (ro + 1) * TAPS] = wv[ro].T
    copies.start(wov, w_out)
    copies.finish()


def halo_rows(sz, halos, band, side):
    other = band - 1 if side == 0 else band + 1
    inside = jnp.logical_and(other >= 0, other < sz.bands)
    vals = halos[jnp.clip(other, 0, sz.bands - 1)].astype(F32)
    return vals * jnp.where(inside, 1.0, 0.0)


def forward_kernel(
    sz, place, e_in, x_in, halos, w3, w_proj, pre_out, hid_out, ext_out, snd_out,
    ext, xv, hv, wv, wpv, pre, hid, snd, es, ps, preds, hr, sems,
):
    width = sz.lon
    pairs = sz.lat // 2
    copies = Copies(sems)
    inner = slice(width, width + sz.pos)
    load_h = copies.start(halos, hv)
    load_w = copies.start(w3, wv)
    load_e = [copies.start(e_in.at[m, :, inner], ext.at[m, :, inner]) for m in range(sz.mem)]
    load_p = copies.start(w_proj, wpv)
    load_x = [copies.start(x_in.at[m], xv.at[m]) for m in range(sz.mem)]
    es[...] = jnp.zeros_like(es)
    if sz.subpad > sz.sub:
        ps[...] = jnp.zeros_like(ps)
    copies.finish([load_h])
    for side in range(2):
        at = 0 if side == 0 else width + sz.pos
        hr[...] = halo_rows(sz, hv, place[1], side)
        for m in range(sz.mem):
            ext[m, :, at : at + width] = expand_row(hr[pl.ds(m * sz.ch, sz.ch), :], es)
    copies.finish([load_w])

    def conv(m, pair):
        cols = jnp.concatenate(
            [ext[m, :, (pair * 2 + ro) * width : (pair * 2 + ro + 2) * width] for ro in range(3)],
            axis=0,
        )
        pre[m, :, pair * 2 * width : (pair + 1) * 2 * width] = jnp.dot(
            wv[...], cols, preferred_element_type=F32
        )

    def rest(m, pair):
        here = slice(pair * 2 * width, (pair + 1) * 2 * width)
        preact = pre[m, :, here]
        hidden = (preact * (1.0 + lax.erf(preact * SQRT_HALF))).astype(BF16)
        hid[m, :, here] = hidden
        pred = xv[m, :, here].astype(F32) + 0.5 * jnp.dot(
            wpv[...], hidden, preferred_element_type=F32
        )
        preds[:, here] = pred.astype(BF16).astype(F32)

    for m in range(sz.mem):
        copies.finish([load_e[m]])
        copies.start(ext.at[m], ext_out.at[m])
        conv(m, 0)
        copies.finish([load_p, load_x[m]])
        for pair in range(pairs):
            if pair + 1 < pairs:
                conv(m, pair + 1)
            rest(m, pair)
            if pair % 2 == 1:
                here = slice((pair - 1) * 2 * width, (pair + 1) * 2 * width)
                copies.start(pre.at[m, :, here], pre_out.at[m, :, here])
                copies.start(hid.at[m, :, here], hid_out.at[m, :, here])
        for prow in range(sz.prows):
            for group in range(sz.groups):
                first = prow * 8 + group * sz.parts
                rows = [
                    preds[:, (first + i) * width : (first + i + 1) * width]
                    for i in range(sz.parts)
                ]
                for q, out in enumerate(swap_blocks(rows)):
                    ps[q, pl.ds(group * sz.ch, sz.ch), :] = out
            for q in range(sz.parts):
                snd[prow * sz.parts + q, m] = ps[q].astype(BF16)
    copies.start(snd, snd_out)
    copies.finish()


def slope_kernel(preact, slope):
    rows = 32

    def one(i, carry):
        at = pl.ds(pl.multiple_of(i * rows, rows), rows)
        x = preact[0, at, :]
        twice = 1.0 + lax.erf(x * SQRT_HALF)
        bell = jnp.exp2(x * x * (-0.5 * LOG2_E)) * (2.0 * INV_ROOT_TWO_PI)
        slope[0, at, :] = twice + x * bell
        return carry

    lax.fori_loop(0, preact.shape[1] // rows, one, 0)


def pair_kernel(sz, count, match, place, preds, truth, grads_out, pv, tv, grads, vals, tsc, sums, scale, inv, sems):
    norm = 1.0 / (32.0 * sz.ch)
    members = sz.members
    folds = sz.subpad // 8
    copies = Copies(sems)
    copies.start(preds, pv)
    copies.start(truth.at[place[0]], tv)
    copies.finish()
    vals[...] = pv[...].reshape(members, sz.subpad, LANES).astype(F32)
    tsc[...] = tv[...].astype(F32)

    def squares(diff):
        return jnp.sum((diff * diff).reshape(folds, 8, LANES), axis=0)

    def first(m, carry):
        own = vals[m]
        sums[pl.ds(pl.multiple_of((count * members + m) * 8, 8), 8), :] = squares(own - tsc[...])
        for k in range(count):
            other = match[k, m]
            inv[k, other] = m
            at = pl.multiple_of((k * members + m) * 8, 8)
            sums[pl.ds(at, 8), :] = squares(own - vals[other])
        return carry

    lax.fori_loop(0, members, first, 0)
    rows = (count + 1) * members
    total = sums[pl.ds(0, rows, stride=8), :]
    for j in range(1, 8):
        total = total + sums[pl.ds(j, rows, stride=8), :]
    step = sz.lon // sz.parts
    while step < LANES:
        total = total + pltpu.roll(total, step, 1)
        step *= 2
    lane = lax.broadcasted_iota(jnp.int32, total.shape, 1)
    for bit in (1, 2):
        total = total + jnp.where(
            (lane & bit) == 0, pltpu.roll(total, LANES - bit, 1), pltpu.roll(total, bit, 1)
        )
    inverse = lax.rsqrt(total * norm + 1e-06)
    scale[pl.ds(0, count * members), :] = inverse[: count * members] * (0.5 / count)
    scale[pl.ds(count * members, members), :] = inverse[count * members :]

    def second(m, carry):
        weight = scale[pl.ds(count * members + m, 1), :]
        acc = None
        own_weight = weight
        for k in range(count):
            back = inv[k, m]
            for other, index in ((match[k, m], k * members + m), (back, k * members + back)):
                part = scale[pl.ds(index, 1), :]
                own_weight = own_weight - part
                term = part * vals[other]
                acc = term if acc is None else acc + term
        out = own_weight * vals[m] + (acc - weight * tsc[...])
        grads[m // sz.mem, m % sz.mem] = out.astype(BF16)
        return carry

    lax.fori_loop(0, members, second, 0)
    copies.start(grads, grads_out)
    copies.finish()


def fold_taps(part, channels):
    return (
        part[channels : 2 * channels]
        + shift_left(part[0:channels])
        + shift_right(part[2 * channels : 3 * channels])
    )


def weight_sums(sz, core, gpre, hid_half, ext, gp, store):
    block = sz.hid // sz.devs

    def take(ref):
        rows = []
        for z in range(sz.devs // 2):
            at = pl.ds(pl.multiple_of((2 * z + core) * block, block), block)
            rows.append(jnp.concatenate([ref[m, at, :] for m in range(sz.mem)], axis=1))
        return jnp.concatenate(rows, axis=0)

    dims = (((1,), (1,)), ((), ()))
    left = take(gpre)
    for ro in range(3):
        cols = [ext[m, :, ro * sz.lon : ro * sz.lon + sz.pos] for m in range(sz.mem)]
        store(
            ro * TAPS,
            lax.dot_general(
                left, jnp.concatenate(cols, axis=1), dims, preferred_element_type=F32
            ),
        )
    cols = [gp[m] for m in range(sz.mem)]
    store(
        3 * TAPS,
        0.5
        * lax.dot_general(
            jnp.concatenate([hid_half[m] for m in range(sz.mem)], axis=1),
            jnp.concatenate(cols, axis=1),
            dims,
            preferred_element_type=F32,
        ),
    )
    store(sz.used, jnp.zeros((sz.hid // 2, sz.cols - sz.used), F32))


def sibling_kernel(
    sz, place, back, slope_in, hid_in, ext, w_proj, wt3,
    gp, gpre, hid, edge_up, edge_dn, sib,
    bv, sv, wpv, wv, rows_f, wpt, hid_sib, sems,
):
    width = sz.lon
    copies = Copies(sems)
    load_b = copies.start(back, bv)
    load_p = copies.start(w_proj, wpv)
    quarter = sz.pos // 4
    load_s = []
    for m in range(sz.mem):
        for part in range(4):
            at = slice(part * quarter, (part + 1) * quarter)
            load_s.append(copies.start(slope_in.at[m, :, at], sv.at[m, :, at]))
    load_w = copies.start(wt3, wv)
    block = sz.hid // sz.devs
    load_h = []
    for half, core in ((hid_sib, 1 - place[2]), (hid, place[2])):
        for m in range(sz.mem):
            for z in range(sz.devs // 2):
                at = pl.ds(pl.multiple_of((2 * z + core) * block, block), block)
                to = slice(z * block, (z + 1) * block)
                load_h.append(copies.start(hid_in.at[m, at, :], half.at[m, to, :]))
    copies.finish([load_p])
    wpt[...] = (wpv[...].astype(F32) * 0.5).T.astype(BF16)
    copies.finish([load_b])
    for m in range(sz.mem):
        for prow in range(sz.prows):
            for q in range(sz.parts):
                rows_f[q] = bv[prow * sz.parts + q, m].astype(F32)
            for group in range(sz.groups):
                outs = swap_blocks(
                    [rows_f[q, pl.ds(group * sz.ch, sz.ch), :] for q in range(sz.parts)]
                )
                for i, out in enumerate(outs):
                    row = prow * 8 + group * sz.parts + i
                    gp[m, :, row * width : (row + 1) * width] = out.astype(BF16)
        for pair in range(sz.lat // 2):
            here = slice(pair * 2 * width, (pair + 1) * 2 * width)
            if here.start % quarter == 0:
                copies.finish([load_s[m * 4 + here.start // quarter]])
            dhid = jnp.dot(wpt[...], gp[m, :, here], preferred_element_type=F32)
            gpre[m, :, here] = (dhid * sv[m, :, here]).astype(BF16)
    copies.finish([load_w])
    for m in range(sz.mem):
        for side, edge in enumerate((edge_up, edge_dn)):
            at = 0 if side == 0 else sz.pos - width
            part = jnp.dot(
                wv[2 * side], gpre[m, :, at : at + width], preferred_element_type=F32
            )
            edge[m] = fold_taps(part, sz.ch)
    copies.finish(load_h[: len(load_h) // 2])

    def store(at, term):
        sib[:, at : at + term.shape[1]] = term.astype(BF16)

    weight_sums(sz, 1 - place[2], gpre, hid_sib, ext, gp, store)
    copies.finish()


def own_kernel(sz, place, gpre, hid, ext, gp, own):
    def store(at, term):
        own[:, at : at + term.shape[1]] = term

    weight_sums(sz, place[2], gpre, hid, ext, gp, store)


def merge_kernel(own, other, out):
    out[...] = (own[...] + other[...].astype(F32)).astype(BF16)


def data_kernel(sz, gpre, gp, wt3, ov, ev, gs):
    width = sz.lon
    for m in range(sz.mem):

        def two_rows(first):
            low, high = max(first, 0), min(first + 2, sz.lat)
            cols = [gpre[m, :, low * width : high * width]]
            zero = jnp.zeros((sz.hid, width), BF16)
            if first < 0:
                cols.insert(0, zero)
            if first + 2 > sz.lat:
                cols.append(zero)
            return cols[0] if len(cols) == 1 else jnp.concatenate(cols, axis=1)

        for pair in range(sz.lat // 2):
            part = None
            for ro in range(3):
                term = jnp.dot(wt3[ro], two_rows(pair * 2 + 1 - ro), preferred_element_type=F32)
                part = term if part is None else part + term
            for i in range(2):
                row = pair * 2 + i
                at = row * width
                total = gp[m, :, at : at + width].astype(F32) + fold_taps(
                    part[:, i * width : (i + 1) * width], sz.ch
                )
                if row in (0, sz.lat - 1):
                    ev[0 if row == 0 else 1, m] = total
                gs[pl.ds(row, sz.ch, stride=sz.lat), :] = total
        ov[m] = gs[...].reshape(sz.ch, sz.lat, width).astype(BF16)


def border_kernel(sz, part, ev, uv, dv, out, ov, gs, sems):
    width = sz.lon
    copies = Copies(sems)
    for m in range(sz.mem):
        gs[...] = part[m].astype(F32).reshape(sz.ch * sz.lat, width)
        gs[pl.ds(0, sz.ch, stride=sz.lat), :] = ev[0, m] + uv[m]
        gs[pl.ds(sz.lat - 1, sz.ch, stride=sz.lat), :] = ev[1, m] + dv[m]
        ov[m] = gs[...].reshape(sz.ch, sz.lat, width).astype(BF16)
        copies.start(ov.at[m], out.at[m])
    copies.finish()


def final_kernel(sz, factor, terms, conv, proj):
    total = terms[0].astype(F32)
    for i in range(1, terms.shape[0]):
        total = total + terms[i].astype(F32)
    total = total * factor
    taps = 3 * sz.ch
    for ro in range(3):
        conv[:, ro * taps : (ro + 1) * taps] = total[:, ro * TAPS : ro * TAPS + taps]
    proj[...] = total[:, 3 * TAPS : sz.used]


MEMBER = ("pair", "core")


def on_device(states, noise_field, target, w_conv, w_proj, matchings):
    member_count = lax.axis_size("pair") * lax.axis_size("core")
    band_count = lax.axis_size("band")
    sz = Sizes(states, w_conv, member_count, band_count)
    mem, ch, lat, lon, hid, pos = sz.mem, sz.ch, sz.lat, sz.lon, sz.hid, sz.pos
    count = matchings.shape[0]
    down = [(i, i + 1) for i in range(band_count - 1)]
    up = [(i + 1, i) for i in range(band_count - 1)]
    band = lax.axis_index("band").astype(jnp.int32)
    core = lax.axis_index("core").astype(jnp.int32)
    member = lax.axis_index("pair").astype(jnp.int32) * lax.axis_size("core") + core
    place = jnp.stack([member, band, core])

    wt3 = jnp.pad(w_conv.T.reshape(3, 3 * ch, hid), ((0, 0), (0, TAPS - 3 * ch), (0, 0)))
    ext_shape = (mem, TAPS, pos + 2 * lon)
    part_shape = (sz.devs, mem, sz.subpad, LANES)
    flat = pltpu.VMEM((ch * lat, lon), F32)
    taps_row = pltpu.VMEM((TAPS, lon), F32)
    regroup_rows = pltpu.VMEM((sz.parts, sz.subpad, LANES), F32)
    wide_bf = pltpu.VMEM((mem, hid, pos), BF16)
    wide_f = pltpu.VMEM((mem, hid, pos), F32)
    rows_bf = pltpu.VMEM((mem, ch, pos), BF16)
    halo_shape = (band_count, mem * ch, lon)

    x_in, send = call(
        functools.partial(inputs_kernel, sz),
        "inputs",
        [((mem, ch, pos), BF16), (halo_shape, BF16)],
        [
            pltpu.VMEM((mem, ch, lat, lon), BF16),
            pltpu.VMEM((mem, ch, lat, lon), F32),
            flat,
            rows_bf,
            pltpu.VMEM(halo_shape, BF16),
            pltpu.VMEM((2, mem * ch, lon), F32),
            dma(3 * mem + 1),
        ],
        1_000_000,
        4_000_000,
        (place, states, noise_field),
        smem=(0,),
    )
    halos = lax.all_to_all(send, "band", 0, 0, tiled=True)
    e_in, truth, w3 = call(
        functools.partial(prep_kernel, sz),
        "prep",
        [(ext_shape, BF16), ((sz.devs, sz.subpad, LANES), BF16), ((hid, 3 * TAPS), BF16)],
        [
            rows_bf,
            pltpu.VMEM((ch, lat, lon), BF16),
            pltpu.VMEM((3, TAPS, hid), BF16),
            pltpu.VMEM((mem, TAPS, pos), BF16),
            pltpu.VMEM((sz.devs, sz.subpad, LANES), BF16),
            pltpu.VMEM((hid, 3 * TAPS), BF16),
            flat,
            taps_row,
            regroup_rows,
            dma(2 * mem + 4),
        ],
        10_000_000,
        8_000_000,
        (x_in, target, wt3),
    )

    conv_flops = 2 * mem * pos * hid * 3 * TAPS
    preact, hidden, ext, snd = call(
        functools.partial(forward_kernel, sz),
        "forward",
        [((mem, hid, pos), F32), ((mem, hid, pos), BF16), (ext_shape, BF16), (part_shape, BF16)],
        [
            pltpu.VMEM(ext_shape, BF16),
            rows_bf,
            pltpu.VMEM(halo_shape, BF16),
            pltpu.VMEM((hid, 3 * TAPS), BF16),
            pltpu.VMEM(w_proj.shape, BF16),
            wide_f,
            wide_bf,
            pltpu.VMEM(part_shape, BF16),
            taps_row,
            regroup_rows,
            pltpu.VMEM((ch, pos), F32),
            pltpu.VMEM((mem * ch, lon), F32),
            dma(4 + 3 * mem + mem * lat // 2),
        ],
        conv_flops,
        9_000_000,
        (place, e_in, x_in, halos, w3, w_proj),
        smem=(0,),
    )

    preds = lax.all_to_all(snd, MEMBER, 0, 0, tiled=True)
    block = pl.BlockSpec((1, hid // 4, pos), lambda m, i: (m, i, 0))
    slope = pl.pallas_call(
        slope_kernel,
        grid=(mem, 4),
        in_specs=[block],
        out_specs=block,
        out_shape=jax.ShapeDtypeStruct((mem, hid, pos), F32),
        compiler_params=pltpu.CompilerParams(vmem_limit_bytes=16 * 1024 * 1024),
        cost_estimate=pl.CostEstimate(
            flops=10 * mem * hid * pos, bytes_accessed=8 * mem * hid * pos, transcendentals=0
        ),
        name="slope",
    )(preact)

    rows = (count + 1) * sz.members
    (grads,) = call(
        functools.partial(pair_kernel, sz, count),
        "pairs",
        [(part_shape, BF16)],
        [
            pltpu.VMEM(part_shape, BF16),
            pltpu.VMEM((sz.subpad, LANES), BF16),
            pltpu.VMEM(part_shape, BF16),
            pltpu.VMEM((sz.members, sz.subpad, LANES), F32),
            pltpu.VMEM((sz.subpad, LANES), F32),
            pltpu.VMEM((rows * 8, LANES), F32),
            pltpu.VMEM((rows, LANES), F32),
            pltpu.SMEM((count, sz.members), jnp.int32),
            dma(3),
        ],
        sz.members * 30 * sz.subpad * LANES,
        2_000_000,
        (matchings, place, preds, truth),
        smem=(0, 1),
    )
    back = lax.all_to_all(grads, MEMBER, 0, 0, tiled=True)

    half = (hid // 2, sz.cols)
    edge_shape = (mem, ch, lon)
    grad_pred, grad_pre, hid_v, edge_up, edge_dn, sibling = call(
        functools.partial(sibling_kernel, sz),
        "sibling",
        [
            ((mem, ch, pos), BF16),
            ((mem, hid, pos), BF16),
            ((mem, hid // 2, pos), BF16),
            (edge_shape, F32),
            (edge_shape, F32),
            (half, BF16),
        ],
        [
            pltpu.VMEM(part_shape, BF16),
            wide_f,
            pltpu.VMEM(w_proj.shape, BF16),
            pltpu.VMEM((3, TAPS, hid), BF16),
            regroup_rows,
            pltpu.VMEM((hid, ch), BF16),
            pltpu.VMEM((mem, hid // 2, pos), BF16),
            dma(3 + 4 * mem + mem * sz.devs),
        ],
        conv_flops,
        9_000_000,
        (place, back, slope, hidden, ext, w_proj, wt3),
        smem=(0,),
        vmem=(4,),
        vmem_outs=range(6),
        limit=40,
    )
    swapped = lax.ppermute(sibling, "core", [(0, 1), (1, 0)])
    (own,) = call(
        functools.partial(own_kernel, sz),
        "own",
        [(half, F32)],
        [],
        conv_flops // 2,
        9_000_000,
        (place, grad_pre, hid_v, ext, grad_pred),
        smem=(0,),
        vmem=range(1, 5),
        vmem_outs=(0,),
        limit=16,
    )
    (partial,) = call(
        merge_kernel,
        "merge",
        [(half, BF16)],
        [],
        500_000,
        2_000_000,
        (own, swapped),
        vmem=(0, 1),
        vmem_outs=(0,),
        limit=16,
    )
    shards = member_count * band_count
    each = hid // shards
    terms = lax.all_to_all(
        partial.reshape(shards // 2, each, sz.cols), ("pair", "band"), 0, 0, tiled=True
    )
    edge_up, edge_dn, _ = lax.optimization_barrier((edge_up, edge_dn, partial))
    from_dn = lax.ppermute(edge_up, "band", up)
    from_up = lax.ppermute(edge_dn, "band", down)

    part_states, edge_sums = call(
        functools.partial(data_kernel, sz),
        "data",
        [((mem, ch, lat, lon), BF16), ((2,) + edge_shape, F32)],
        [flat],
        conv_flops,
        8_000_000,
        (grad_pre, grad_pred, wt3),
        vmem=range(3),
        vmem_outs=(0, 1),
        limit=16,
    )
    (grad_states,) = call(
        functools.partial(border_kernel, sz),
        "border",
        [((mem, ch, lat, lon), BF16)],
        [
            pltpu.VMEM((mem, ch, lat, lon), BF16),
            flat,
            dma(mem),
        ],
        1_000_000,
        2_000_000,
        (part_states, edge_sums, from_up, from_dn),
        vmem=range(4),
        limit=16,
    )

    factor = 1.0 / (pos * sz.members * band_count) ** 0.5
    grad_conv, grad_proj = call(
        functools.partial(final_kernel, sz, factor),
        "final",
        [((each, 9 * ch), F32), ((each, ch), F32)],
        [],
        500_000,
        500_000,
        (terms,),
        vmem=(0,),
        vmem_outs=(0, 1),
        limit=16,
    )
    return grad_states, grad_conv, grad_proj.T


def solution(mesh):
    members = mesh.shape["member"]
    split = jax.sharding.Mesh(
        mesh.devices.reshape(members // 2, 2, mesh.shape["band"]), MEMBER + ("band",)
    )
    return jax.shard_map(
        on_device,
        mesh=split,
        in_specs=(
            P(MEMBER, None, "band", None),
            P(MEMBER, None, "band", None),
            P(None, "band", None),
            P(),
            P(),
            P(),
        ),
        out_specs=(
            P(MEMBER, None, "band", None),
            P(MEMBER + ("band",), None),
            P(None, MEMBER + ("band",)),
        ),
        check_vma=False,
    )
```

```python
import functools

import jax
import jax.numpy as jnp
from jax import lax
from jax.experimental import pallas as pl
from jax.experimental.pallas import tpu as pltpu
from jax.sharding import PartitionSpec as P

SQRT_HALF = 0.7071067811865476
INV_ROOT_TWO_PI = 0.3989422804014327
F32 = jnp.float32
BF16 = jnp.bfloat16
LANES = 128
TAPS = 256
LOG2_E = 1.4426950408889634


def call(
    kernel, name, outs, scratch, flops, moved, args,
    smem=(), vmem=(), vmem_outs=(), limit=60, aliases=None,
):
    kinds = {"hbm": pltpu.HBM, "vmem": pltpu.VMEM, "smem": pltpu.SMEM}
    specs = {kind: pl.BlockSpec(memory_space=space) for kind, space in kinds.items()}

    def kind(i):
        return "smem" if i in smem else "vmem" if i in vmem else "hbm"

    return pl.pallas_call(
        kernel,
        in_specs=[specs[kind(i)] for i in range(len(args))],
        out_specs=[specs["vmem" if i in vmem_outs else "hbm"] for i in range(len(outs))],
        out_shape=[jax.ShapeDtypeStruct(*out) for out in outs],
        scratch_shapes=scratch,
        input_output_aliases=aliases or {},
        compiler_params=pltpu.CompilerParams(vmem_limit_bytes=limit * 1024 * 1024),
        cost_estimate=pl.CostEstimate(flops=flops, bytes_accessed=moved, transcendentals=0),
        name=name,
    )(*args)


class Copies:
    def __init__(self, sems):
        self.sems, self.used, self.open = sems, 0, []

    def start(self, src, dst):
        copy = pltpu.make_async_copy(src, dst, self.sems.at[self.used])
        self.used += 1
        copy.start()
        self.open.append(copy)
        return copy

    def finish(self, copies=None):
        for copy in list(self.open) if copies is None else copies:
            if any(copy is other for other in self.open):
                self.open = [other for other in self.open if other is not copy]
                copy.wait()


def dma(count):
    return pltpu.SemaphoreType.DMA((count,))


def shift_right(vals):
    lane = lax.broadcasted_iota(jnp.int32, vals.shape, 1)
    return jnp.where(lane == 0, 0.0, pltpu.roll(vals, 1, 1))


def shift_left(vals):
    width = vals.shape[1]
    lane = lax.broadcasted_iota(jnp.int32, vals.shape, 1)
    return jnp.where(lane == width - 1, 0.0, pltpu.roll(vals, width - 1, 1))


def expand_row(vals, scratch):
    channels = vals.shape[0]
    scratch[pl.ds(0, channels), :] = shift_right(vals)
    scratch[pl.ds(channels, channels), :] = vals
    scratch[pl.ds(2 * channels, channels), :] = shift_left(vals)
    return scratch[...].astype(BF16)


def swap_blocks(rows):
    parts = len(rows)
    size = rows[0].shape[1] // parts
    lane = lax.broadcasted_iota(jnp.int32, rows[0].shape, 1)
    rows = list(rows)
    bit = 1
    while bit < parts:
        low = (lane & (bit * size)) == 0
        shift = bit * size
        width = rows[0].shape[1]
        for i in range(parts):
            if i & bit:
                continue
            a, b = rows[i], rows[i | bit]
            rows[i] = jnp.where(low, a, pltpu.roll(b, shift, 1))
            rows[i | bit] = jnp.where(low, pltpu.roll(a, width - shift, 1), b)
        bit *= 2
    return rows


class Sizes:
    def __init__(self, states, w_conv, member_count, band_count):
        self.mem, self.ch, self.lat, self.lon = states.shape
        self.hid = w_conv.shape[0]
        self.devs = member_count
        self.bands = band_count
        self.members = self.mem * member_count
        self.prows = self.lat // 8
        self.parts = member_count // self.prows
        self.groups = 8 // self.parts
        self.sub = self.groups * self.ch
        self.subpad = (self.sub + 7) // 8 * 8
        self.pos = self.lat * self.lon
        self.used = 3 * TAPS + self.ch
        self.cols = (self.used + LANES - 1) // LANES * LANES


def edges_kernel(sz, place, states, noise, send, st, ns, xs, sv, rows, sems):
    copies = Copies(sems)
    loads = []
    for m in range(sz.mem):
        loads.append(
            [copies.start(states.at[m], st.at[m]), copies.start(noise.at[m], ns.at[m])]
        )
    for m in range(sz.mem):
        copies.finish(loads[m])
        at = pl.ds(m * sz.ch, sz.ch)
        for side, tile in enumerate((0, sz.lat - 8)):
            xs[...] = st[m, :, tile : tile + 8, :].astype(F32).reshape(sz.ch * 8, sz.lon)
            row = xs[pl.ds(0 if side == 0 else 7, sz.ch, stride=8), :]
            noise_rows = ns.at[m]
            rows[side, at, :] = row + noise_rows[:, 0 if side == 0 else sz.lat - 1, :]
    for other in range(sz.bands):
        after = jnp.where(other > place[1], 1.0, 0.0)
        sv[other] = (rows[1] * after + rows[0] * (1.0 - after)).astype(BF16)
    copies.start(sv, send)
    copies.finish()


def prep_kernel(
    sz, states, noise, w_t, x_out, e_out, w_out, wt3_out,
    st, ns, wv, xv, ev, wov, wt3v, xs, es, sems,
):
    copies = Copies(sems)
    w_load = copies.start(w_t, wv)
    loads = []
    for m in range(sz.mem):
        loads.append(
            [copies.start(states.at[m], st.at[m]), copies.start(noise.at[m], ns.at[m])]
        )
    es[...] = jnp.zeros_like(es)
    inner = slice(sz.lon, sz.lon + sz.pos)
    taps = 3 * sz.ch
    copies.finish([w_load])
    for ro in range(3):
        piece = jnp.concatenate(
            [wv[ro * taps : (ro + 1) * taps, :], jnp.zeros((TAPS - taps, sz.hid), BF16)], axis=0
        )
        wt3v[ro] = piece
        wov[:, ro * TAPS : (ro + 1) * TAPS] = piece.T
    copies.start(wov, w_out)
    copies.start(wt3v, wt3_out)
    for m in range(sz.mem):
        copies.finish(loads[m])
        xs[...] = (st[m].astype(F32) + ns[m]).astype(BF16).astype(F32).reshape(
            sz.ch * sz.lat, sz.lon
        )
        for row in range(sz.lat):
            here = slice(row * sz.lon, (row + 1) * sz.lon)
            vals = xs[pl.ds(row, sz.ch, stride=sz.lat), :]
            xv[m, :, here] = vals.astype(BF16)
            ev[m, :, here] = expand_row(vals, es)
        copies.start(ev.at[m], e_out.at[m, :, inner])
        copies.start(xv.at[m], x_out.at[m])
    copies.finish()


def truth_kernel(sz, target, t_out, xs, ps):
    xs[...] = target[...].astype(F32).reshape(sz.ch * sz.lat, sz.lon)
    if sz.subpad > sz.sub:
        ps[...] = jnp.zeros_like(ps)
    for prow in range(sz.prows):
        for group in range(sz.groups):
            first = prow * 8 + group * sz.parts
            rows = [xs[pl.ds(first + i, sz.ch, stride=sz.lat), :] for i in range(sz.parts)]
            for q, out in enumerate(swap_blocks(rows)):
                ps[q, pl.ds(group * sz.ch, sz.ch), :] = out
        for q in range(sz.parts):
            t_out[prow * sz.parts + q] = ps[q].astype(BF16)


def halo_rows(sz, halos, band, side):
    other = band - 1 if side == 0 else band + 1
    inside = jnp.logical_and(other >= 0, other < sz.bands)
    vals = halos[jnp.clip(other, 0, sz.bands - 1)].astype(F32)
    return vals * jnp.where(inside, 1.0, 0.0)


def forward_kernel(
    sz, place, e_in, x_in, halos, w3, w_proj, pre_out, hid_out, ext_out, snd_out,
    ext, xv, hv, wv, wpv, pre, preb, hid, snd, es, ps, preds, hr, hx, sems,
):
    width = sz.lon
    pairs = sz.lat // 2
    copies = Copies(sems)
    inner = slice(width, width + sz.pos)
    load_h = copies.start(halos, hv)
    load_e = [copies.start(e_in.at[0, :, inner], ext.at[0, :, inner])]
    load_w = copies.start(w3, wv)
    for m in range(1, sz.mem):
        load_e.append(copies.start(e_in.at[m, :, inner], ext.at[m, :, inner]))
    load_p = copies.start(w_proj, wpv)
    load_x = [copies.start(x_in.at[m], xv.at[m]) for m in range(sz.mem)]
    es[...] = jnp.zeros_like(es)
    if sz.subpad > sz.sub:
        ps[...] = jnp.zeros_like(ps)
    copies.finish([load_h])
    for side in range(2):
        at = 0 if side == 0 else width + sz.pos
        hr[...] = halo_rows(sz, hv, place[1], side)
        for m in range(sz.mem):
            row = expand_row(hr[pl.ds(m * sz.ch, sz.ch), :], es)
            ext[m, :, at : at + width] = row
            hx[side, m] = row
    for side in range(2):
        at = 0 if side == 0 else width + sz.pos
        copies.start(hx.at[side], ext_out.at[:, :, at : at + width])
    copies.finish([load_w])

    def conv(m, pair):
        cols = jnp.concatenate(
            [ext[m, :, (pair * 2 + ro) * width : (pair * 2 + ro + 2) * width] for ro in range(3)],
            axis=0,
        )
        pre[pair % 2] = jnp.dot(wv[...], cols, preferred_element_type=F32)

    def rest(m, pair):
        here = slice(pair * 2 * width, (pair + 1) * 2 * width)
        preact = pre[pair % 2]
        preb[m, :, here] = preact.astype(BF16)
        hidden = (preact * (1.0 + lax.erf(preact * SQRT_HALF))).astype(BF16)
        hid[m, :, here] = hidden
        pred = xv[m, :, here].astype(F32) + 0.5 * jnp.dot(
            wpv[...], hidden, preferred_element_type=F32
        )
        preds[:, here] = pred.astype(BF16).astype(F32)

    for m in range(sz.mem):
        copies.finish([load_e[m]])
        conv(m, 0)
        copies.finish([load_p, load_x[m]])
        for pair in range(pairs):
            if pair + 1 < pairs:
                conv(m, pair + 1)
            rest(m, pair)
            if pair % 2 == 1:
                here = slice((pair - 1) * 2 * width, (pair + 1) * 2 * width)
                copies.start(preb.at[m, :, here], pre_out.at[m, :, here])
                copies.start(hid.at[m, :, here], hid_out.at[m, :, here])
        for prow in range(sz.prows):
            for group in range(sz.groups):
                first = prow * 8 + group * sz.parts
                rows = [
                    preds[:, (first + i) * width : (first + i + 1) * width]
                    for i in range(sz.parts)
                ]
                for q, out in enumerate(swap_blocks(rows)):
                    ps[q, pl.ds(group * sz.ch, sz.ch), :] = out
            for q in range(sz.parts):
                snd[m, prow * sz.parts + q] = ps[q].astype(BF16)
        copies.start(snd.at[m], snd_out.at[:, m])
    copies.finish()


def slope_kernel(preact, slope):
    rows = 32

    def one(i, carry):
        at = pl.ds(pl.multiple_of(i * rows, rows), rows)
        x = preact[0, at, :].astype(F32)
        twice = 1.0 + lax.erf(x * SQRT_HALF)
        bell = jnp.exp2(x * x * (-0.5 * LOG2_E)) * (2.0 * INV_ROOT_TWO_PI)
        slope[0, at, :] = twice + x * bell
        return carry

    lax.fori_loop(0, preact.shape[1] // rows, one, 0)


def pair_kernel(sz, count, match, place, preds, truth, grads_out, grads, vals, tsc, sums, scale, inv, sems):
    norm = 1.0 / (32.0 * sz.ch)
    members = sz.members
    folds = sz.subpad // 8
    copies = Copies(sems)
    vals[...] = preds[...].reshape(members, sz.subpad, LANES).astype(F32)
    tsc[...] = truth[place[0]].astype(F32)

    def squares(diff):
        return jnp.sum((diff * diff).reshape(folds, 8, LANES), axis=0)

    def first(m, carry):
        own = vals[m]
        sums[pl.ds(pl.multiple_of((count * members + m) * 8, 8), 8), :] = squares(own - tsc[...])
        for k in range(count):
            other = match[k, m]
            inv[k, other] = m
            at = pl.multiple_of((k * members + m) * 8, 8)
            sums[pl.ds(at, 8), :] = squares(own - vals[other])
        return carry

    lax.fori_loop(0, members, first, 0)
    rows = (count + 1) * members
    total = sums[pl.ds(0, rows, stride=8), :]
    for j in range(1, 8):
        total = total + sums[pl.ds(j, rows, stride=8), :]
    step = sz.lon // sz.parts
    while step < LANES:
        total = total + pltpu.roll(total, step, 1)
        step *= 2
    lane = lax.broadcasted_iota(jnp.int32, total.shape, 1)
    for bit in (1, 2):
        total = total + jnp.where(
            (lane & bit) == 0, pltpu.roll(total, LANES - bit, 1), pltpu.roll(total, bit, 1)
        )
    inverse = lax.rsqrt(total * norm + 1e-06)
    scale[pl.ds(0, count * members), :] = inverse[: count * members] * (0.5 / count)
    scale[pl.ds(count * members, members), :] = inverse[count * members :]

    def second(m):
        weight = scale[pl.ds(count * members + m, 1), :]
        acc = None
        own_weight = weight
        for k in range(count):
            back = inv[k, m]
            for other, index in ((match[k, m], k * members + m), (back, k * members + back)):
                part = scale[pl.ds(index, 1), :]
                own_weight = own_weight - part
                term = part * vals[other]
                acc = term if acc is None else acc + term
        return (own_weight * vals[m] + (acc - weight * tsc[...])).astype(BF16)

    quarter = sz.devs // 4
    for part in range(4):

        def several(i, carry):
            m = part * (members // 4) + i
            grads[m // sz.mem, m % sz.mem] = second(m)
            return carry

        lax.fori_loop(0, members // 4, several, 0)
        at = slice(part * quarter, (part + 1) * quarter)
        copies.start(grads.at[at], grads_out.at[at])
    copies.finish()


def fold_taps(part, channels):
    return (
        part[channels : 2 * channels]
        + shift_left(part[0:channels])
        + shift_right(part[2 * channels : 3 * channels])
    )


def weight_sums(sz, core, gpre, hid_half, ext, gp, store):
    block = sz.hid // sz.devs

    def take(ref):
        rows = []
        for z in range(sz.devs // 2):
            at = pl.ds(pl.multiple_of((2 * z + core) * block, block), block)
            rows.append(jnp.concatenate([ref[m, at, :] for m in range(sz.mem)], axis=1))
        return jnp.concatenate(rows, axis=0)

    dims = (((1,), (1,)), ((), ()))
    left = take(gpre)
    for ro in range(3):
        cols = [ext[m, :, ro * sz.lon : ro * sz.lon + sz.pos] for m in range(sz.mem)]
        store(
            ro * TAPS,
            lax.dot_general(
                left, jnp.concatenate(cols, axis=1), dims, preferred_element_type=F32
            ),
        )
    cols = [gp[m] for m in range(sz.mem)]
    store(
        3 * TAPS,
        0.5
        * lax.dot_general(
            jnp.concatenate([hid_half[m] for m in range(sz.mem)], axis=1),
            jnp.concatenate(cols, axis=1),
            dims,
            preferred_element_type=F32,
        ),
    )
    store(sz.used, jnp.zeros((sz.hid // 2, sz.cols - sz.used), F32))


def sibling_kernel(
    sz, place, back, slope_in, hid_in, ext, w_proj, wt3_in, gp, gpre, hid, edge_up, edge_dn, sib,
    slope, hid_sib, wt3, rows_f, wpt, sems,
):
    width = sz.lon
    copies = Copies(sems)
    quarter = sz.pos // 4
    load_s = []
    for m in range(sz.mem):
        for part in range(4):
            at = slice(part * quarter, (part + 1) * quarter)
            load_s.append(copies.start(slope_in.at[m, :, at], slope.at[m, :, at]))
    load_w = copies.start(wt3_in, wt3)
    block = sz.hid // sz.devs
    load_h = []
    for half, core in ((hid_sib, 1 - place[2]), (hid, place[2])):
        for m in range(sz.mem):
            for z in range(sz.devs // 2):
                at = pl.ds(pl.multiple_of((2 * z + core) * block, block), block)
                to = slice(z * block, (z + 1) * block)
                load_h.append(copies.start(hid_in.at[m, at, :], half.at[m, to, :]))
    wpt[...] = (w_proj[...].astype(F32) * 0.5).T.astype(BF16)
    for m in range(sz.mem):
        for prow in range(sz.prows):
            for q in range(sz.parts):
                rows_f[q] = back[prow * sz.parts + q, m].astype(F32)
            for group in range(sz.groups):
                outs = swap_blocks(
                    [rows_f[q, pl.ds(group * sz.ch, sz.ch), :] for q in range(sz.parts)]
                )
                for i, out in enumerate(outs):
                    row = prow * 8 + group * sz.parts + i
                    gp[m, :, row * width : (row + 1) * width] = out.astype(BF16)
        for pair in range(sz.lat // 2):
            here = slice(pair * 2 * width, (pair + 1) * 2 * width)
            if here.start % quarter == 0:
                copies.finish([load_s[m * 4 + here.start // quarter]])
            dhid = jnp.dot(wpt[...], gp[m, :, here], preferred_element_type=F32)
            gpre[m, :, here] = (dhid * slope[m, :, here]).astype(BF16)
    copies.finish([load_w])
    for m in range(sz.mem):
        for side, edge in enumerate((edge_up, edge_dn)):
            at = 0 if side == 0 else sz.pos - width
            part = jnp.dot(
                wt3[2 * side], gpre[m, :, at : at + width], preferred_element_type=F32
            )
            edge[m] = fold_taps(part, sz.ch)

    def store(at, term):
        sib[:, at : at + term.shape[1]] = term.astype(BF16)

    copies.finish(load_h[: len(load_h) // 2])
    weight_sums(sz, 1 - place[2], gpre, hid_sib, ext, gp, store)
    copies.finish()


def own_kernel(sz, place, gpre, hid, ext, gp, own):
    def store(at, term):
        own[:, at : at + term.shape[1]] = term

    weight_sums(sz, place[2], gpre, hid, ext, gp, store)


def merge_kernel(own, other, out):
    out[...] = (own[...] + other[...].astype(F32)).astype(BF16)


def data_kernel(sz, gpre, gp, wt3, ov, ev, gs):
    width = sz.lon
    for m in range(sz.mem):

        def two_rows(first):
            low, high = max(first, 0), min(first + 2, sz.lat)
            cols = [gpre[m, :, low * width : high * width]]
            zero = jnp.zeros((sz.hid, width), BF16)
            if first < 0:
                cols.insert(0, zero)
            if first + 2 > sz.lat:
                cols.append(zero)
            return cols[0] if len(cols) == 1 else jnp.concatenate(cols, axis=1)

        for pair in range(sz.lat // 2):
            part = None
            for ro in range(3):
                term = jnp.dot(wt3[ro], two_rows(pair * 2 + 1 - ro), preferred_element_type=F32)
                part = term if part is None else part + term
            for i in range(2):
                row = pair * 2 + i
                at = row * width
                total = gp[m, :, at : at + width].astype(F32) + fold_taps(
                    part[:, i * width : (i + 1) * width], sz.ch
                )
                if row in (0, sz.lat - 1):
                    ev[0 if row == 0 else 1, m] = total
                gs[pl.ds(row, sz.ch, stride=sz.lat), :] = total
        ov[m] = gs[...].reshape(sz.ch, sz.lat, width).astype(BF16)


def border_kernel(sz, part, ev, uv, dv, out, ov, gs, sems):
    width = sz.lon
    copies = Copies(sems)
    for m in range(sz.mem):
        gs[...] = part[m].astype(F32).reshape(sz.ch * sz.lat, width)
        gs[pl.ds(0, sz.ch, stride=sz.lat), :] = ev[0, m] + uv[m]
        gs[pl.ds(sz.lat - 1, sz.ch, stride=sz.lat), :] = ev[1, m] + dv[m]
        ov[m] = gs[...].reshape(sz.ch, sz.lat, width).astype(BF16)
        copies.start(ov.at[m], out.at[m])
    copies.finish()


def final_kernel(sz, factor, terms, conv, proj):
    total = terms[0].astype(F32)
    for i in range(1, terms.shape[0]):
        total = total + terms[i].astype(F32)
    total = total * factor
    taps = 3 * sz.ch
    for ro in range(3):
        conv[:, ro * taps : (ro + 1) * taps] = total[:, ro * TAPS : ro * TAPS + taps]
    proj[...] = total[:, 3 * TAPS : sz.used]


MEMBER = ("pair", "core")


def on_device(states, noise_field, target, w_conv, w_proj, matchings):
    member_count = lax.axis_size("pair") * lax.axis_size("core")
    band_count = lax.axis_size("band")
    sz = Sizes(states, w_conv, member_count, band_count)
    mem, ch, lat, lon, hid, pos = sz.mem, sz.ch, sz.lat, sz.lon, sz.hid, sz.pos
    count = matchings.shape[0]
    down = [(i, i + 1) for i in range(band_count - 1)]
    up = [(i + 1, i) for i in range(band_count - 1)]
    band = lax.axis_index("band").astype(jnp.int32)
    core = lax.axis_index("core").astype(jnp.int32)
    member = lax.axis_index("pair").astype(jnp.int32) * lax.axis_size("core") + core
    place = jnp.stack([member, band, core])

    ext_shape = (mem, TAPS, pos + 2 * lon)
    part_shape = (sz.devs, mem, sz.subpad, LANES)
    flat = pltpu.VMEM((ch * lat, lon), F32)
    taps_row = pltpu.VMEM((TAPS, lon), F32)
    regroup_rows = pltpu.VMEM((sz.parts, sz.subpad, LANES), F32)
    wide_bf = pltpu.VMEM((mem, hid, pos), BF16)
    rows_bf = pltpu.VMEM((mem, ch, pos), BF16)
    halo_shape = (band_count, mem * ch, lon)

    both_bf = pltpu.VMEM((mem, ch, lat, lon), BF16)
    both_f = pltpu.VMEM((mem, ch, lat, lon), F32)
    (send,) = call(
        functools.partial(edges_kernel, sz),
        "edges",
        [(halo_shape, BF16)],
        [
            both_bf,
            both_f,
            pltpu.VMEM((ch * 8, lon), F32),
            pltpu.VMEM(halo_shape, BF16),
            pltpu.VMEM((2, mem * ch, lon), F32),
            dma(2 * mem + 1),
        ],
        1_000_000,
        3_000_000,
        (place, states, noise_field),
        smem=(0,),
    )
    halos = lax.all_to_all(send, "band", 0, 0, tiled=True)
    x_in, e_in, w3, wt3 = call(
        functools.partial(prep_kernel, sz),
        "prep",
        [((mem, ch, pos), BF16), (ext_shape, BF16), ((hid, 3 * TAPS), BF16), ((3, TAPS, hid), BF16)],
        [
            both_bf,
            both_f,
            pltpu.VMEM((9 * ch, hid), BF16),
            rows_bf,
            pltpu.VMEM((mem, TAPS, pos), BF16),
            pltpu.VMEM((hid, 3 * TAPS), BF16),
            pltpu.VMEM((3, TAPS, hid), BF16),
            flat,
            taps_row,
            dma(4 * mem + 3),
        ],
        10_000_000,
        8_000_000,
        (states, noise_field, w_conv.T),
    )

    conv_flops = 2 * mem * pos * hid * 3 * TAPS
    preact, hidden, ext, snd = call(
        functools.partial(forward_kernel, sz),
        "forward",
        [((mem, hid, pos), BF16), ((mem, hid, pos), BF16), (ext_shape, BF16), (part_shape, BF16)],
        [
            pltpu.VMEM(ext_shape, BF16),
            rows_bf,
            pltpu.VMEM(halo_shape, BF16),
            pltpu.VMEM((hid, 3 * TAPS), BF16),
            pltpu.VMEM(w_proj.shape, BF16),
            pltpu.VMEM((2, hid, 2 * lon), F32),
            wide_bf,
            wide_bf,
            pltpu.VMEM((mem, sz.devs, sz.subpad, LANES), BF16),
            taps_row,
            regroup_rows,
            pltpu.VMEM((ch, pos), F32),
            pltpu.VMEM((mem * ch, lon), F32),
            pltpu.VMEM((2, mem, TAPS, lon), BF16),
            dma(5 + 3 * mem + mem * lat // 2),
        ],
        conv_flops,
        9_000_000,
        (place, e_in, x_in, halos, w3, w_proj),
        smem=(0,),
        aliases={1: 2},
    )

    preds = lax.all_to_all(snd, MEMBER, 0, 0, tiled=True)
    late_target, _ = lax.optimization_barrier((target, snd))
    (truth,) = call(
        functools.partial(truth_kernel, sz),
        "truth",
        [((sz.devs, sz.subpad, LANES), BF16)],
        [flat, regroup_rows],
        5_000_000,
        2_000_000,
        (late_target,),
        vmem=(0,),
        vmem_outs=(0,),
        limit=16,
    )
    block = pl.BlockSpec((1, hid // 4, pos), lambda m, i: (m, i, 0))
    slope = pl.pallas_call(
        slope_kernel,
        grid=(mem, 4),
        in_specs=[block],
        out_specs=block,
        out_shape=jax.ShapeDtypeStruct((mem, hid, pos), F32),
        compiler_params=pltpu.CompilerParams(vmem_limit_bytes=16 * 1024 * 1024),
        cost_estimate=pl.CostEstimate(
            flops=10 * mem * hid * pos, bytes_accessed=8 * mem * hid * pos, transcendentals=0
        ),
        name="slope",
    )(preact)

    rows = (count + 1) * sz.members
    (grads,) = call(
        functools.partial(pair_kernel, sz, count),
        "pairs",
        [(part_shape, BF16)],
        [
            pltpu.VMEM(part_shape, BF16),
            pltpu.VMEM((sz.members, sz.subpad, LANES), F32),
            pltpu.VMEM((sz.subpad, LANES), F32),
            pltpu.VMEM((rows * 8, LANES), F32),
            pltpu.VMEM((rows, LANES), F32),
            pltpu.SMEM((count, sz.members), jnp.int32),
            dma(4),
        ],
        sz.members * 30 * sz.subpad * LANES,
        2_000_000,
        (matchings, place, preds, truth),
        smem=(0, 1),
        vmem=(2, 3),
        limit=16,
    )
    back = lax.all_to_all(grads, MEMBER, 0, 0, tiled=True)

    half = (hid // 2, sz.cols)
    edge_shape = (mem, ch, lon)
    grad_pred, grad_pre, hid_own, edge_up, edge_dn, sibling = call(
        functools.partial(sibling_kernel, sz),
        "sibling",
        [
            ((mem, ch, pos), BF16),
            ((mem, hid, pos), BF16),
            ((mem, hid // 2, pos), BF16),
            (edge_shape, F32),
            (edge_shape, F32),
            (half, BF16),
        ],
        [
            pltpu.VMEM((mem, hid, pos), F32),
            pltpu.VMEM((mem, hid // 2, pos), BF16),
            pltpu.VMEM((3, TAPS, hid), BF16),
            regroup_rows,
            pltpu.VMEM((hid, ch), BF16),
            dma(1 + 4 * mem + mem * sz.devs),
        ],
        conv_flops,
        9_000_000,
        (place, back, slope, hidden, ext, w_proj, wt3),
        smem=(0,),
        vmem=(1, 4, 5),
        vmem_outs=range(6),
        limit=40,
    )
    swapped = lax.ppermute(sibling, "core", [(0, 1), (1, 0)])
    (own,) = call(
        functools.partial(own_kernel, sz),
        "own",
        [(half, F32)],
        [],
        conv_flops // 2,
        9_000_000,
        (place, grad_pre, hid_own, ext, grad_pred),
        smem=(0,),
        vmem=range(1, 5),
        vmem_outs=(0,),
        limit=16,
    )
    (partial,) = call(
        merge_kernel,
        "merge",
        [(half, BF16)],
        [],
        500_000,
        2_000_000,
        (own, swapped),
        vmem=(0, 1),
        vmem_outs=(0,),
        limit=16,
    )
    shards = member_count * band_count
    each = hid // shards
    terms = lax.all_to_all(
        partial.reshape(shards // 2, each, sz.cols), ("pair", "band"), 0, 0, tiled=True
    )
    edge_up, edge_dn, _ = lax.optimization_barrier((edge_up, edge_dn, partial))
    from_dn = lax.ppermute(edge_up, "band", up)
    from_up = lax.ppermute(edge_dn, "band", down)

    part_states, edge_sums = call(
        functools.partial(data_kernel, sz),
        "data",
        [((mem, ch, lat, lon), BF16), ((2,) + edge_shape, F32)],
        [flat],
        conv_flops,
        8_000_000,
        (grad_pre, grad_pred, wt3),
        vmem=range(3),
        vmem_outs=(0, 1),
        limit=16,
    )
    (grad_states,) = call(
        functools.partial(border_kernel, sz),
        "border",
        [((mem, ch, lat, lon), BF16)],
        [
            pltpu.VMEM((mem, ch, lat, lon), BF16),
            flat,
            dma(mem),
        ],
        1_000_000,
        2_000_000,
        (part_states, edge_sums, from_up, from_dn),
        vmem=range(4),
        limit=16,
    )

    factor = 1.0 / (pos * sz.members * band_count) ** 0.5
    grad_conv, grad_proj = call(
        functools.partial(final_kernel, sz, factor),
        "final",
        [((each, 9 * ch), F32), ((each, ch), F32)],
        [],
        500_000,
        500_000,
        (terms,),
        vmem=(0,),
        vmem_outs=(0, 1),
        limit=16,
    )
    return grad_states, grad_conv, grad_proj.T


def solution(mesh):
    members = mesh.shape["member"]
    split = jax.sharding.Mesh(
        mesh.devices.reshape(members // 2, 2, mesh.shape["band"]), MEMBER + ("band",)
    )
    return jax.shard_map(
        on_device,
        mesh=split,
        in_specs=(
            P(MEMBER, None, "band", None),
            P(MEMBER, None, "band", None),
            P(None, "band", None),
            P(),
            P(),
            P(),
        ),
        out_specs=(
            P(MEMBER, None, "band", None),
            P(MEMBER + ("band",), None),
            P(None, MEMBER + ("band",)),
        ),
        check_vma=False,
    )
```

```python
import functools

import jax
import jax.numpy as jnp
from jax import lax
from jax.experimental import pallas as pl
from jax.experimental.pallas import tpu as pltpu
from jax.sharding import PartitionSpec as P

SQRT_HALF = 0.7071067811865476
INV_ROOT_TWO_PI = 0.3989422804014327
F32 = jnp.float32
BF16 = jnp.bfloat16
LANES = 128
TAPS = 256
LOG2_E = 1.4426950408889634


def call(
    kernel, name, outs, scratch, flops, moved, args,
    smem=(), vmem=(), vmem_outs=(), limit=60, aliases=None,
):
    kinds = {"hbm": pltpu.HBM, "vmem": pltpu.VMEM, "smem": pltpu.SMEM}
    specs = {kind: pl.BlockSpec(memory_space=space) for kind, space in kinds.items()}

    def kind(i):
        return "smem" if i in smem else "vmem" if i in vmem else "hbm"

    return pl.pallas_call(
        kernel,
        in_specs=[specs[kind(i)] for i in range(len(args))],
        out_specs=[specs["vmem" if i in vmem_outs else "hbm"] for i in range(len(outs))],
        out_shape=[jax.ShapeDtypeStruct(*out) for out in outs],
        scratch_shapes=scratch,
        input_output_aliases=aliases or {},
        compiler_params=pltpu.CompilerParams(vmem_limit_bytes=limit * 1024 * 1024),
        cost_estimate=pl.CostEstimate(flops=flops, bytes_accessed=moved, transcendentals=0),
        name=name,
    )(*args)


class Copies:
    def __init__(self, sems):
        self.sems, self.used, self.open = sems, 0, []

    def start(self, src, dst):
        copy = pltpu.make_async_copy(src, dst, self.sems.at[self.used])
        self.used += 1
        copy.start()
        self.open.append(copy)
        return copy

    def finish(self, copies=None):
        for copy in list(self.open) if copies is None else copies:
            if any(copy is other for other in self.open):
                self.open = [other for other in self.open if other is not copy]
                copy.wait()


def dma(count):
    return pltpu.SemaphoreType.DMA((count,))


def shift_right(vals):
    lane = lax.broadcasted_iota(jnp.int32, vals.shape, 1)
    return jnp.where(lane == 0, 0.0, pltpu.roll(vals, 1, 1))


def shift_left(vals):
    width = vals.shape[1]
    lane = lax.broadcasted_iota(jnp.int32, vals.shape, 1)
    return jnp.where(lane == width - 1, 0.0, pltpu.roll(vals, width - 1, 1))


def expand_row(vals, scratch):
    channels = vals.shape[0]
    scratch[pl.ds(0, channels), :] = shift_right(vals)
    scratch[pl.ds(channels, channels), :] = vals
    scratch[pl.ds(2 * channels, channels), :] = shift_left(vals)
    return scratch[...].astype(BF16)


def swap_blocks(rows):
    parts = len(rows)
    size = rows[0].shape[1] // parts
    lane = lax.broadcasted_iota(jnp.int32, rows[0].shape, 1)
    rows = list(rows)
    bit = 1
    while bit < parts:
        low = (lane & (bit * size)) == 0
        shift = bit * size
        width = rows[0].shape[1]
        for i in range(parts):
            if i & bit:
                continue
            a, b = rows[i], rows[i | bit]
            rows[i] = jnp.where(low, a, pltpu.roll(b, shift, 1))
            rows[i | bit] = jnp.where(low, pltpu.roll(a, width - shift, 1), b)
        bit *= 2
    return rows


class Sizes:
    def __init__(self, states, w_conv, member_count, band_count):
        self.mem, self.ch, self.lat, self.lon = states.shape
        self.hid = w_conv.shape[0]
        self.devs = member_count
        self.bands = band_count
        self.members = self.mem * member_count
        self.prows = self.lat // 8
        self.parts = member_count // self.prows
        self.groups = 8 // self.parts
        self.sub = self.groups * self.ch
        self.subpad = (self.sub + 7) // 8 * 8
        self.pos = self.lat * self.lon
        self.used = 3 * TAPS + self.ch
        self.cols = (self.used + LANES - 1) // LANES * LANES


def edges_kernel(sz, states, noise, send, st, ns, xs, sv, rows, sems):
    copies = Copies(sems)
    loads = []
    for m in range(sz.mem):
        loads.append(
            [copies.start(states.at[m], st.at[m]), copies.start(noise.at[m], ns.at[m])]
        )
    for m in range(sz.mem):
        copies.finish(loads[m])
        at = pl.ds(m * sz.ch, sz.ch)
        for side, tile in enumerate((0, sz.lat - 8)):
            xs[...] = st[m, :, tile : tile + 8, :].astype(F32).reshape(sz.ch * 8, sz.lon)
            row = xs[pl.ds(0 if side == 0 else 7, sz.ch, stride=8), :]
            noise_rows = ns.at[m]
            rows[side, at, :] = row + noise_rows[:, 0 if side == 0 else sz.lat - 1, :]
    for other in range(sz.bands):
        after = jnp.where(other > lax.axis_index("band"), 1.0, 0.0)
        sv[other] = (rows[1] * after + rows[0] * (1.0 - after)).astype(BF16)
    copies.start(sv, send)
    copies.finish()


def conv_pair(sz, ext, w3, m, pair):
    width = sz.lon
    cols = jnp.concatenate(
        [ext[m, :, (pair * 2 + ro) * width : (pair * 2 + ro + 2) * width] for ro in range(3)],
        axis=0,
    )
    return jnp.dot(w3[...], cols, preferred_element_type=F32)


def hidden_pair(preact):
    return (preact * (1.0 + lax.erf(preact * SQRT_HALF))).astype(BF16)


def project_pair(x, w_proj, hidden):
    pred = x.astype(F32) + 0.5 * jnp.dot(w_proj[...], hidden, preferred_element_type=F32)
    return pred.astype(BF16).astype(F32)


def front_kernel(
    sz, states, noise, w_t, w_proj, pre_out, hid_out, ext_out, preds_out, w3_out, wt3_out,
    st, ns, wv, xv, pre, preb, hid, ext, preds, w3, wt3v, xs, es, sems,
):
    copies = Copies(sems)
    width = sz.lon
    loads = []
    for m in range(sz.mem):
        loads.append(
            [copies.start(states.at[m], st.at[m]), copies.start(noise.at[m], ns.at[m])]
        )
        if m == 0:
            w_load = copies.start(w_t, wv)
    es[...] = jnp.zeros_like(es)
    taps = 3 * sz.ch
    last = sz.lat // 2 - 1

    def expand(m):
        copies.finish(loads[m])
        xs[...] = (st[m].astype(F32) + ns[m]).astype(BF16).astype(F32).reshape(
            sz.ch * sz.lat, sz.lon
        )
        for row in range(sz.lat):
            vals = xs[pl.ds(row, sz.ch, stride=sz.lat), :]
            xv[:, row * width : (row + 1) * width] = vals
            ext[m, :, (row + 1) * width : (row + 2) * width] = expand_row(vals, es)

    def rest(m, pair):
        here = slice(pair * 2 * width, (pair + 1) * 2 * width)
        preact = pre[pair % 2]
        preb[m, :, here] = preact.astype(BF16)
        hidden = hidden_pair(preact)
        hid[m, :, here] = hidden
        preds[m, :, here] = project_pair(xv[:, here], w_proj, hidden)

    for m in range(sz.mem):
        expand(m)
        if m == 0:
            copies.finish([w_load])
            for ro in range(3):
                piece = jnp.concatenate(
                    [
                        wv[ro * taps : (ro + 1) * taps, :],
                        jnp.zeros((TAPS - taps, sz.hid), BF16),
                    ],
                    axis=0,
                )
                wt3v[ro] = piece
                w3[:, ro * TAPS : (ro + 1) * TAPS] = piece.T
            copies.start(w3, w3_out)
            copies.start(wt3v, wt3_out)
        inner = slice(width, width + sz.pos)
        copies.start(ext.at[m, :, inner], ext_out.at[m, :, inner])
        pre[1] = conv_pair(sz, ext, w3, m, 1)
        for pair in range(1, last):
            if pair + 1 < last:
                pre[(pair + 1) % 2] = conv_pair(sz, ext, w3, m, pair + 1)
            rest(m, pair)
            if pair % 2 == 0 or pair + 1 == last:
                first = pair if pair % 2 else pair - 1
                here = slice(first * 2 * width, (pair + 1) * 2 * width)
                copies.start(preb.at[m, :, here], pre_out.at[m, :, here])
                copies.start(hid.at[m, :, here], hid_out.at[m, :, here])
        here = slice(2 * width, sz.pos - 2 * width)
        copies.start(preds.at[m, :, here], preds_out.at[m, :, here])
    copies.finish()


def truth_kernel(sz, target, t_out, xs, ps):
    xs[...] = target[...].astype(F32).reshape(sz.ch * sz.lat, sz.lon)
    if sz.subpad > sz.sub:
        ps[...] = jnp.zeros_like(ps)
    for prow in range(sz.prows):
        for group in range(sz.groups):
            first = prow * 8 + group * sz.parts
            rows = [xs[pl.ds(first + i, sz.ch, stride=sz.lat), :] for i in range(sz.parts)]
            for q, out in enumerate(swap_blocks(rows)):
                ps[q, pl.ds(group * sz.ch, sz.ch), :] = out
        for q in range(sz.parts):
            t_out[prow * sz.parts + q] = ps[q].astype(BF16)


def halo_rows(sz, halos, side):
    band = lax.axis_index("band")
    other = band - 1 if side == 0 else band + 1
    inside = jnp.logical_and(other >= 0, other < sz.bands)
    vals = halos[jnp.clip(other, 0, sz.bands - 1)].astype(F32)
    return vals * jnp.where(inside, 1.0, 0.0)


def rim_kernel(
    sz, halos_in, pre_in, hid_in, ext_in, preds_in, w3_in, w_proj_in,
    pre_out, hid_out, ext_out, snd_out,
    pre, preb, hid, snd, halos, ends, preds, w3, w_proj, xf, rim, es, ps, hr, sems,
):
    width = sz.lon
    copies = Copies(sems)
    load_h = copies.start(halos_in, halos)
    load_w = copies.start(w3_in, w3)
    load_e = []
    for side in range(2):
        at = width if side == 0 else sz.pos - 2 * width
        to = width if side == 0 else 0
        load_e.append(
            copies.start(
                ext_in.at[:, :, at : at + 3 * width], ends.at[side, :, :, to : to + 3 * width]
            )
        )
    load_p = copies.start(w_proj_in, w_proj)
    here = slice(2 * width, sz.pos - 2 * width)
    load_f = [copies.start(preds_in.at[m, :, here], preds.at[m, :, here]) for m in range(sz.mem)]
    es[...] = jnp.zeros_like(es)
    if sz.subpad > sz.sub:
        ps[...] = jnp.zeros_like(ps)
    copies.finish([load_h])
    for side in range(2):
        at = 0 if side == 0 else 3 * width
        hr[...] = halo_rows(sz, halos, side)
        for m in range(sz.mem):
            ends[side, m, :, at : at + width] = expand_row(hr[pl.ds(m * sz.ch, sz.ch), :], es)
        to = 0 if side == 0 else width + sz.pos
        copies.start(ends.at[side, :, :, at : at + width], ext_out.at[:, :, to : to + width])
    copies.finish([load_w] + load_e)
    last = sz.lat // 2 - 1
    units = [(m, side) for m in range(sz.mem) for side in range(2)]

    def conv(i):
        m, side = units[i]
        pre[i % 2] = conv_pair(sz, ends.at[side], w3, m, 0)

    conv(0)
    copies.finish([load_p])
    for i, (m, side) in enumerate(units):
        if i + 1 < len(units):
            conv(i + 1)
        here = slice(side * last * 2 * width, (side * last + 1) * 2 * width)
        preact = pre[i % 2]
        preb[i] = preact.astype(BF16)
        hidden = hidden_pair(preact)
        hid[i] = hidden
        copies.start(preb.at[i], pre_out.at[m, :, here])
        copies.start(hid.at[i], hid_out.at[m, :, here])
        xf[...] = ends[side, m, :, width : 3 * width].astype(F32)
        rim[side] = project_pair(xf[pl.ds(sz.ch, sz.ch), :], w_proj, hidden)
        if side == 0:
            continue
        copies.finish([load_f[m]])

        def row_of(row):
            if row < 2 or row >= sz.lat - 2:
                at = row % 2 * width
                return rim[0 if row < 2 else 1, :, at : at + width]
            return preds[m, :, row * width : (row + 1) * width]

        for prow in range(sz.prows):
            for group in range(sz.groups):
                first = prow * 8 + group * sz.parts
                rows = [row_of(first + k) for k in range(sz.parts)]
                for q, out in enumerate(swap_blocks(rows)):
                    ps[q, pl.ds(group * sz.ch, sz.ch), :] = out
            for q in range(sz.parts):
                snd[m, prow * sz.parts + q] = ps[q].astype(BF16)
        copies.start(snd.at[m], snd_out.at[:, m])
    copies.finish()


def slope_kernel(preact, slope):
    rows = 32

    def one(i, carry):
        at = pl.ds(pl.multiple_of(i * rows, rows), rows)
        x = preact[0, at, :].astype(F32)
        twice = 1.0 + lax.erf(x * SQRT_HALF)
        bell = jnp.exp2(x * x * (-0.5 * LOG2_E)) * (2.0 * INV_ROOT_TWO_PI)
        slope[0, at, :] = (twice + x * bell).astype(BF16)
        return carry

    lax.fori_loop(0, preact.shape[1] // rows, one, 0)


def pair_kernel(sz, count, match, preds, truth, grads_out, grads, vals, tsc, sums, scale, inv, sems):
    norm = 1.0 / (32.0 * sz.ch)
    members = sz.members
    folds = sz.subpad // 8
    copies = Copies(sems)
    vals[...] = preds[...].reshape(members, sz.subpad, LANES).astype(F32)
    tsc[...] = truth[lax.axis_index("pair") * 2 + lax.axis_index("core")].astype(F32)

    def squares(diff):
        return jnp.sum((diff * diff).reshape(folds, 8, LANES), axis=0)

    def first(m, carry):
        own = vals[m]
        sums[pl.ds(pl.multiple_of((count * members + m) * 8, 8), 8), :] = squares(own - tsc[...])
        for k in range(count):
            other = match[k, m]
            inv[k, other] = m
            at = pl.multiple_of((k * members + m) * 8, 8)
            sums[pl.ds(at, 8), :] = squares(own - vals[other])
        return carry

    lax.fori_loop(0, members, first, 0)
    rows = (count + 1) * members
    total = sums[pl.ds(0, rows, stride=8), :]
    for j in range(1, 8):
        total = total + sums[pl.ds(j, rows, stride=8), :]
    step = sz.lon // sz.parts
    while step < LANES:
        total = total + pltpu.roll(total, step, 1)
        step *= 2
    lane = lax.broadcasted_iota(jnp.int32, total.shape, 1)
    for bit in (1, 2):
        total = total + jnp.where(
            (lane & bit) == 0, pltpu.roll(total, LANES - bit, 1), pltpu.roll(total, bit, 1)
        )
    inverse = lax.rsqrt(total * norm + 1e-06)
    scale[pl.ds(0, count * members), :] = inverse[: count * members] * (0.5 / count)
    scale[pl.ds(count * members, members), :] = inverse[count * members :]

    def second(m):
        weight = scale[pl.ds(count * members + m, 1), :]
        acc = None
        own_weight = weight
        for k in range(count):
            back = inv[k, m]
            for other, index in ((match[k, m], k * members + m), (back, k * members + back)):
                part = scale[pl.ds(index, 1), :]
                own_weight = own_weight - part
                term = part * vals[other]
                acc = term if acc is None else acc + term
        return (own_weight * vals[m] + (acc - weight * tsc[...])).astype(BF16)

    quarter = sz.devs // 4
    for part in range(4):

        def several(i, carry):
            m = part * (members // 4) + i
            grads[m // sz.mem, m % sz.mem] = second(m)
            return carry

        lax.fori_loop(0, members // 4, several, 0)
        at = slice(part * quarter, (part + 1) * quarter)
        copies.start(grads.at[at], grads_out.at[at])
    copies.finish()


def fold_taps(part, channels):
    return (
        part[channels : 2 * channels]
        + shift_left(part[0:channels])
        + shift_right(part[2 * channels : 3 * channels])
    )


def weight_sums(sz, core, gpre, hid_half, ext, gp, store):
    block = sz.hid // sz.devs

    def take(ref):
        rows = []
        for z in range(sz.devs // 2):
            at = pl.ds(pl.multiple_of((2 * z + core) * block, block), block)
            rows.append(jnp.concatenate([ref[m, at, :] for m in range(sz.mem)], axis=1))
        return jnp.concatenate(rows, axis=0)

    dims = (((1,), (1,)), ((), ()))
    left = take(gpre)
    for ro in range(3):
        cols = [ext[m, :, ro * sz.lon : ro * sz.lon + sz.pos] for m in range(sz.mem)]
        store(
            ro * TAPS,
            lax.dot_general(
                left, jnp.concatenate(cols, axis=1), dims, preferred_element_type=F32
            ),
        )
    cols = [gp[m] for m in range(sz.mem)]
    store(
        3 * TAPS,
        0.5
        * lax.dot_general(
            jnp.concatenate([hid_half[m] for m in range(sz.mem)], axis=1),
            jnp.concatenate(cols, axis=1),
            dims,
            preferred_element_type=F32,
        ),
    )
    store(sz.used, jnp.zeros((sz.hid // 2, sz.cols - sz.used), F32))


def sibling_kernel(
    sz, back_in, slope_in, hid_in, ext, w_proj, gp, gpre, hid, sib,
    back, slope, hid_sib, rows_f, wpt, sems,
):
    width = sz.lon
    copies = Copies(sems)
    load_b = copies.start(back_in, back)
    quarter = sz.pos // 4
    load_s = []
    for m in range(sz.mem):
        for part in range(4):
            at = slice(part * quarter, (part + 1) * quarter)
            load_s.append(copies.start(slope_in.at[m, :, at], slope.at[m, :, at]))
    block = sz.hid // sz.devs
    mine = lax.axis_index("core")
    load_h = []
    for half, core in ((hid_sib, 1 - mine), (hid, mine)):
        for m in range(sz.mem):
            for z in range(sz.devs // 2):
                at = pl.ds(pl.multiple_of((2 * z + core) * block, block), block)
                to = slice(z * block, (z + 1) * block)
                load_h.append(copies.start(hid_in.at[m, at, :], half.at[m, to, :]))
    wpt[...] = (w_proj[...].astype(F32) * 0.5).T.astype(BF16)
    copies.finish([load_b])
    for m in range(sz.mem):
        for prow in range(sz.prows):
            for q in range(sz.parts):
                rows_f[q] = back[prow * sz.parts + q, m].astype(F32)
            for group in range(sz.groups):
                outs = swap_blocks(
                    [rows_f[q, pl.ds(group * sz.ch, sz.ch), :] for q in range(sz.parts)]
                )
                for i, out in enumerate(outs):
                    row = prow * 8 + group * sz.parts + i
                    gp[m, :, row * width : (row + 1) * width] = out.astype(BF16)
        for pair in range(sz.lat // 2):
            here = slice(pair * 2 * width, (pair + 1) * 2 * width)
            if here.start % quarter == 0:
                copies.finish([load_s[m * 4 + here.start // quarter]])
            dhid = jnp.dot(wpt[...], gp[m, :, here], preferred_element_type=F32)
            gpre[m, :, here] = (dhid * slope[m, :, here].astype(F32)).astype(BF16)
    def store(at, term):
        sib[:, at : at + term.shape[1]] = term.astype(BF16)

    copies.finish(load_h[: len(load_h) // 2])
    weight_sums(sz, 1 - mine, gpre, hid_sib, ext, gp, store)
    copies.finish()


def own_kernel(sz, gpre, hid, ext, gp, own):
    def store(at, term):
        own[:, at : at + term.shape[1]] = term

    weight_sums(sz, lax.axis_index("core"), gpre, hid, ext, gp, store)


def merge_kernel(own, other, out):
    out[...] = (own[...] + other[...].astype(F32)).astype(BF16)


def edge_terms_kernel(sz, gpre, wt3_in, edge_up, edge_dn, gv, wt3, sems):
    width = sz.lon
    copies = Copies(sems)
    for side in range(2):
        at = slice(0, width) if side == 0 else slice(sz.pos - width, sz.pos)
        copies.start(wt3_in.at[2 * side], wt3.at[side])
        copies.start(gpre.at[:, :, at], gv.at[side])
    copies.finish()
    for side, edge in enumerate((edge_up, edge_dn)):
        for m in range(sz.mem):
            part = jnp.dot(wt3[side], gv[side, m], preferred_element_type=F32)
            edge[m] = fold_taps(part, sz.ch)


def data_kernel(sz, gpre_in, gp_in, wt3_in, ov, ev, gpre, gp, wt3, gs, sems):
    width = sz.lon
    copies = Copies(sems)
    load_w = copies.start(wt3_in, wt3)
    half = sz.pos // 2
    loads, load_p = [], []
    for m in range(sz.mem):
        for part in range(2):
            at = slice(part * half, (part + 1) * half)
            loads.append(copies.start(gpre_in.at[m, :, at], gpre.at[m, :, at]))
            if part == 0:
                load_p.append(copies.start(gp_in.at[m], gp.at[m]))
    zero = jnp.zeros((sz.hid, width), BF16)
    copies.finish([load_w])
    for m in range(sz.mem):
        copies.finish([loads[2 * m], load_p[m]])

        def two_rows(first):
            low, high = max(first, 0), min(first + 2, sz.lat)
            cols = [gpre[m, :, low * width : high * width]]
            if first < 0:
                cols.insert(0, zero)
            if first + 2 > sz.lat:
                cols.append(zero)
            return cols[0] if len(cols) == 1 else jnp.concatenate(cols, axis=1)

        for pair in range(sz.lat // 2):
            if (pair * 2 + 3) * width > half:
                copies.finish([loads[2 * m + 1]])
            part = None
            for ro in range(3):
                term = jnp.dot(wt3[ro], two_rows(pair * 2 + 1 - ro), preferred_element_type=F32)
                part = term if part is None else part + term
            for i in range(2):
                row = pair * 2 + i
                at = row * width
                total = gp[m, :, at : at + width].astype(F32) + fold_taps(
                    part[:, i * width : (i + 1) * width], sz.ch
                )
                if row in (0, sz.lat - 1):
                    ev[0 if row == 0 else 1, m] = total
                gs[pl.ds(row, sz.ch, stride=sz.lat), :] = total
        ov[m] = gs[...].reshape(sz.ch, sz.lat, width).astype(BF16)


def border_kernel(sz, part, ev, uv, dv, out, ov, gs, sems):
    width = sz.lon
    copies = Copies(sems)
    for m in range(sz.mem):
        gs[...] = part[m].astype(F32).reshape(sz.ch * sz.lat, width)
        gs[pl.ds(0, sz.ch, stride=sz.lat), :] = ev[0, m] + uv[m]
        gs[pl.ds(sz.lat - 1, sz.ch, stride=sz.lat), :] = ev[1, m] + dv[m]
        ov[m] = gs[...].reshape(sz.ch, sz.lat, width).astype(BF16)
        copies.start(ov.at[m], out.at[m])
    copies.finish()


def final_kernel(sz, factor, terms, conv, proj):
    total = terms[0].astype(F32)
    for i in range(1, terms.shape[0]):
        total = total + terms[i].astype(F32)
    total = total * factor
    taps = 3 * sz.ch
    for ro in range(3):
        conv[:, ro * taps : (ro + 1) * taps] = total[:, ro * TAPS : ro * TAPS + taps]
    proj[...] = total[:, 3 * TAPS : sz.used]


MEMBER = ("pair", "core")


def on_device(states, noise_field, target, w_conv, w_proj, matchings):
    member_count = lax.axis_size("pair") * lax.axis_size("core")
    band_count = lax.axis_size("band")
    sz = Sizes(states, w_conv, member_count, band_count)
    mem, ch, lat, lon, hid, pos = sz.mem, sz.ch, sz.lat, sz.lon, sz.hid, sz.pos
    count = matchings.shape[0]
    down = [(i, i + 1) for i in range(band_count - 1)]
    up = [(i + 1, i) for i in range(band_count - 1)]
    ext_shape = (mem, TAPS, pos + 2 * lon)
    part_shape = (sz.devs, mem, sz.subpad, LANES)
    flat = pltpu.VMEM((ch * lat, lon), F32)
    taps_row = pltpu.VMEM((TAPS, lon), F32)
    regroup_rows = pltpu.VMEM((sz.parts, sz.subpad, LANES), F32)
    wide_bf = pltpu.VMEM((mem, hid, pos), BF16)
    halo_shape = (band_count, mem * ch, lon)

    both_bf = pltpu.VMEM((mem, ch, lat, lon), BF16)
    both_f = pltpu.VMEM((mem, ch, lat, lon), F32)
    (send,) = call(
        functools.partial(edges_kernel, sz),
        "edges",
        [(halo_shape, BF16)],
        [
            both_bf,
            both_f,
            pltpu.VMEM((ch * 8, lon), F32),
            pltpu.VMEM(halo_shape, BF16),
            pltpu.VMEM((2, mem * ch, lon), F32),
            dma(2 * mem + 1),
        ],
        1_000_000,
        3_000_000,
        (states, noise_field),
    )
    halos = lax.all_to_all(send, "band", 0, 0, tiled=True)
    conv_flops = 2 * mem * pos * hid * 3 * TAPS
    wide = (mem, hid, pos)
    pair_shape = (hid, 2 * lon)
    preact, hidden, ext, fields, w3, wt3 = call(
        functools.partial(front_kernel, sz),
        "front",
        [
            (wide, BF16),
            (wide, BF16),
            (ext_shape, BF16),
            ((mem, ch, pos), F32),
            ((hid, 3 * TAPS), BF16),
            ((3, TAPS, hid), BF16),
        ],
        [
            both_bf,
            both_f,
            pltpu.VMEM((9 * ch, hid), BF16),
            pltpu.VMEM((ch, pos), F32),
            pltpu.VMEM((2,) + pair_shape, F32),
            wide_bf,
            wide_bf,
            pltpu.VMEM(ext_shape, BF16),
            pltpu.VMEM((mem, ch, pos), F32),
            pltpu.VMEM((hid, 3 * TAPS), BF16),
            pltpu.VMEM((3, TAPS, hid), BF16),
            flat,
            taps_row,
            dma(3 + 4 * mem + mem * lat // 2),
        ],
        conv_flops,
        9_000_000,
        (states, noise_field, w_conv.T, w_proj),
        vmem=(3,),
        limit=55,
    )
    units = 2 * mem
    preact, hidden, ext, snd = call(
        functools.partial(rim_kernel, sz),
        "rim",
        [(wide, BF16), (wide, BF16), (ext_shape, BF16), (part_shape, BF16)],
        [
            pltpu.VMEM((2,) + pair_shape, F32),
            pltpu.VMEM((units,) + pair_shape, BF16),
            pltpu.VMEM((units,) + pair_shape, BF16),
            pltpu.VMEM((mem, sz.devs, sz.subpad, LANES), BF16),
            pltpu.VMEM(halo_shape, BF16),
            pltpu.VMEM((2, mem, TAPS, 4 * lon), BF16),
            pltpu.VMEM((mem, ch, pos), F32),
            pltpu.VMEM((hid, 3 * TAPS), BF16),
            pltpu.VMEM(w_proj.shape, BF16),
            pltpu.VMEM((TAPS, 2 * lon), F32),
            pltpu.VMEM((2, ch, 2 * lon), F32),
            taps_row,
            regroup_rows,
            pltpu.VMEM((mem * ch, lon), F32),
            dma(7 + 2 * units + 2 * mem),
        ],
        conv_flops // 4,
        9_000_000,
        (halos, preact, hidden, ext, fields, w3, w_proj),
        limit=53,
        aliases={1: 0, 2: 1, 3: 2},
    )

    preds = lax.all_to_all(snd, MEMBER, 0, 0, tiled=True)
    late_target, _ = lax.optimization_barrier((target, snd))
    (truth,) = call(
        functools.partial(truth_kernel, sz),
        "truth",
        [((sz.devs, sz.subpad, LANES), BF16)],
        [flat, regroup_rows],
        5_000_000,
        2_000_000,
        (late_target,),
        vmem=(0,),
        vmem_outs=(0,),
        limit=16,
    )
    block = pl.BlockSpec((1, hid // 4, pos), lambda m, i: (m, i, 0))
    slope = pl.pallas_call(
        slope_kernel,
        grid=(mem, 4),
        in_specs=[block],
        out_specs=block,
        out_shape=jax.ShapeDtypeStruct((mem, hid, pos), BF16),
        compiler_params=pltpu.CompilerParams(vmem_limit_bytes=40 * 1024 * 1024),
        cost_estimate=pl.CostEstimate(
            flops=10 * mem * hid * pos, bytes_accessed=8 * mem * hid * pos, transcendentals=0
        ),
        name="slope",
    )(preact)

    rows = (count + 1) * sz.members
    (grads,) = call(
        functools.partial(pair_kernel, sz, count),
        "pairs",
        [(part_shape, BF16)],
        [
            pltpu.VMEM(part_shape, BF16),
            pltpu.VMEM((sz.members, sz.subpad, LANES), F32),
            pltpu.VMEM((sz.subpad, LANES), F32),
            pltpu.VMEM((rows * 8, LANES), F32),
            pltpu.VMEM((rows, LANES), F32),
            pltpu.SMEM((count, sz.members), jnp.int32),
            dma(4),
        ],
        sz.members * 30 * sz.subpad * LANES,
        2_000_000,
        (matchings, preds, truth),
        smem=(0,),
        vmem=(1, 2),
        limit=16,
    )
    back = lax.all_to_all(grads, MEMBER, 0, 0, tiled=True)

    half = (hid // 2, sz.cols)
    edge_shape = (mem, ch, lon)
    grad_pred, grad_pre, hid_own, sibling = call(
        functools.partial(sibling_kernel, sz),
        "sibling",
        [
            ((mem, ch, pos), BF16),
            ((mem, hid, pos), BF16),
            ((mem, hid // 2, pos), BF16),
            (half, BF16),
        ],
        [
            pltpu.VMEM(part_shape, BF16),
            pltpu.VMEM((mem, hid, pos), BF16),
            pltpu.VMEM((mem, hid // 2, pos), BF16),
            regroup_rows,
            pltpu.VMEM((hid, ch), BF16),
            dma(1 + 4 * mem + mem * sz.devs),
        ],
        conv_flops,
        9_000_000,
        (back, slope, hidden, ext, w_proj),
        vmem=(0, 3, 4),
        vmem_outs=range(4),
        limit=40,
    )
    swapped = lax.ppermute(sibling, "core", [(0, 1), (1, 0)])
    (own,) = call(
        functools.partial(own_kernel, sz),
        "own",
        [(half, F32)],
        [],
        conv_flops // 2,
        9_000_000,
        (grad_pre, hid_own, ext, grad_pred),
        vmem=range(4),
        vmem_outs=(0,),
        limit=16,
    )
    (partial,) = call(
        merge_kernel,
        "merge",
        [(half, BF16)],
        [],
        500_000,
        2_000_000,
        (own, swapped),
        vmem=(0, 1),
        vmem_outs=(0,),
        limit=16,
    )
    shards = member_count * band_count
    each = hid // shards
    terms = lax.all_to_all(
        partial.reshape(shards // 2, each, sz.cols), ("pair", "band"), 0, 0, tiled=True
    )
    late_wt3, _ = lax.optimization_barrier((wt3, partial))
    edge_up, edge_dn = call(
        functools.partial(edge_terms_kernel, sz),
        "edge_terms",
        [(edge_shape, F32), (edge_shape, F32)],
        [
            pltpu.VMEM((2, mem, hid, lon), BF16),
            pltpu.VMEM((2, TAPS, hid), BF16),
            dma(4),
        ],
        200_000_000,
        1_500_000,
        (grad_pre, late_wt3),
        vmem_outs=(0, 1),
        limit=60,
    )
    from_dn = lax.ppermute(edge_up, "band", up)
    from_up = lax.ppermute(edge_dn, "band", down)

    part_states, edge_sums = call(
        functools.partial(data_kernel, sz),
        "data",
        [((mem, ch, lat, lon), BF16), ((2,) + edge_shape, F32)],
        [
            wide_bf,
            pltpu.VMEM((mem, ch, pos), BF16),
            pltpu.VMEM((3, TAPS, hid), BF16),
            flat,
            dma(1 + 3 * mem),
        ],
        conv_flops,
        8_000_000,
        (grad_pre, grad_pred, late_wt3),
        vmem_outs=(0, 1),
        limit=50,
    )
    (grad_states,) = call(
        functools.partial(border_kernel, sz),
        "border",
        [((mem, ch, lat, lon), BF16)],
        [
            pltpu.VMEM((mem, ch, lat, lon), BF16),
            flat,
            dma(mem),
        ],
        1_000_000,
        2_000_000,
        (part_states, edge_sums, from_up, from_dn),
        vmem=range(4),
        limit=16,
    )

    factor = 1.0 / (pos * sz.members * band_count) ** 0.5
    grad_conv, grad_proj = call(
        functools.partial(final_kernel, sz, factor),
        "final",
        [((each, 9 * ch), F32), ((each, ch), F32)],
        [],
        500_000,
        500_000,
        (terms,),
        vmem=(0,),
        vmem_outs=(0, 1),
        limit=16,
    )
    return grad_states, grad_conv, grad_proj.T


def solution(mesh):
    members = mesh.shape["member"]
    split = jax.sharding.Mesh(
        mesh.devices.reshape(members // 2, 2, mesh.shape["band"]), MEMBER + ("band",)
    )
    return jax.shard_map(
        on_device,
        mesh=split,
        in_specs=(
            P(MEMBER, None, "band", None),
            P(MEMBER, None, "band", None),
            P(None, "band", None),
            P(),
            P(),
            P(),
        ),
        out_specs=(
            P(MEMBER, None, "band", None),
            P(MEMBER + ("band",), None),
            P(None, MEMBER + ("band",)),
        ),
        check_vma=False,
    )
```

```python
import functools

import jax
import jax.numpy as jnp
from jax import lax
from jax.experimental import pallas as pl
from jax.experimental.pallas import tpu as pltpu
from jax.sharding import PartitionSpec as P

SQRT_HALF = 0.7071067811865476
INV_ROOT_TWO_PI = 0.3989422804014327
F32 = jnp.float32
BF16 = jnp.bfloat16
LANES = 128
TAPS = 256
LOG2_E = 1.4426950408889634


def call(
    kernel, name, outs, scratch, flops, moved, args,
    smem=(), vmem=(), vmem_outs=(), limit=60, aliases=None,
):
    kinds = {"hbm": pltpu.HBM, "vmem": pltpu.VMEM, "smem": pltpu.SMEM}
    specs = {kind: pl.BlockSpec(memory_space=space) for kind, space in kinds.items()}

    def kind(i):
        return "smem" if i in smem else "vmem" if i in vmem else "hbm"

    return pl.pallas_call(
        kernel,
        in_specs=[specs[kind(i)] for i in range(len(args))],
        out_specs=[specs["vmem" if i in vmem_outs else "hbm"] for i in range(len(outs))],
        out_shape=[jax.ShapeDtypeStruct(*out) for out in outs],
        scratch_shapes=scratch,
        input_output_aliases=aliases or {},
        compiler_params=pltpu.CompilerParams(vmem_limit_bytes=limit * 1024 * 1024),
        cost_estimate=pl.CostEstimate(flops=flops, bytes_accessed=moved, transcendentals=0),
        name=name,
    )(*args)


class Copies:
    def __init__(self, sems):
        self.sems, self.used, self.open = sems, 0, []

    def start(self, src, dst):
        copy = pltpu.make_async_copy(src, dst, self.sems.at[self.used])
        self.used += 1
        copy.start()
        self.open.append(copy)
        return copy

    def finish(self, copies=None):
        for copy in list(self.open) if copies is None else copies:
            if any(copy is other for other in self.open):
                self.open = [other for other in self.open if other is not copy]
                copy.wait()


def dma(count):
    return pltpu.SemaphoreType.DMA((count,))


def shift_right(vals):
    lane = lax.broadcasted_iota(jnp.int32, vals.shape, 1)
    return jnp.where(lane == 0, 0.0, pltpu.roll(vals, 1, 1))


def shift_left(vals):
    width = vals.shape[1]
    lane = lax.broadcasted_iota(jnp.int32, vals.shape, 1)
    return jnp.where(lane == width - 1, 0.0, pltpu.roll(vals, width - 1, 1))


def expand_row(vals, scratch):
    channels = vals.shape[0]
    scratch[pl.ds(0, channels), :] = shift_right(vals)
    scratch[pl.ds(channels, channels), :] = vals
    scratch[pl.ds(2 * channels, channels), :] = shift_left(vals)
    return scratch[...].astype(BF16)


def swap_blocks(rows):
    parts = len(rows)
    size = rows[0].shape[1] // parts
    lane = lax.broadcasted_iota(jnp.int32, rows[0].shape, 1)
    rows = list(rows)
    bit = 1
    while bit < parts:
        low = (lane & (bit * size)) == 0
        shift = bit * size
        width = rows[0].shape[1]
        for i in range(parts):
            if i & bit:
                continue
            a, b = rows[i], rows[i | bit]
            rows[i] = jnp.where(low, a, pltpu.roll(b, shift, 1))
            rows[i | bit] = jnp.where(low, pltpu.roll(a, width - shift, 1), b)
        bit *= 2
    return rows


class Sizes:
    def __init__(self, states, w_conv, member_count, band_count):
        self.mem, self.ch, self.lat, self.lon = states.shape
        self.hid = w_conv.shape[0]
        self.devs = member_count
        self.bands = band_count
        self.members = self.mem * member_count
        self.prows = self.lat // 8
        self.parts = member_count // self.prows
        self.groups = 8 // self.parts
        self.sub = self.groups * self.ch
        self.subpad = (self.sub + 7) // 8 * 8
        self.pos = self.lat * self.lon
        self.used = 3 * TAPS + self.ch
        self.cols = (self.used + LANES - 1) // LANES * LANES


def edges_kernel(sz, states, noise, send, st, ns, xs, sv, rows, sems):
    copies = Copies(sems)
    loads = []
    for m in range(sz.mem):
        loads.append(
            [copies.start(states.at[m], st.at[m]), copies.start(noise.at[m], ns.at[m])]
        )
    for m in range(sz.mem):
        copies.finish(loads[m])
        at = pl.ds(m * sz.ch, sz.ch)
        for side, tile in enumerate((0, sz.lat - 8)):
            xs[...] = st[m, :, tile : tile + 8, :].astype(F32).reshape(sz.ch * 8, sz.lon)
            row = xs[pl.ds(0 if side == 0 else 7, sz.ch, stride=8), :]
            noise_rows = ns.at[m]
            rows[side, at, :] = row + noise_rows[:, 0 if side == 0 else sz.lat - 1, :]
    for other in range(sz.bands):
        after = jnp.where(other > lax.axis_index("band"), 1.0, 0.0)
        sv[other] = (rows[1] * after + rows[0] * (1.0 - after)).astype(BF16)
    copies.start(sv, send)
    copies.finish()


def conv_pair(sz, ext, w3, m, pair):
    width = sz.lon
    cols = jnp.concatenate(
        [ext[m, :, (pair * 2 + ro) * width : (pair * 2 + ro + 2) * width] for ro in range(3)],
        axis=0,
    )
    return jnp.dot(w3[...], cols, preferred_element_type=F32)


def hidden_pair(preact):
    return (preact * (1.0 + lax.erf(preact * SQRT_HALF))).astype(BF16)


def project_pair(x, w_proj, hidden):
    pred = x.astype(F32) + 0.5 * jnp.dot(w_proj[...], hidden, preferred_element_type=F32)
    return pred.astype(BF16).astype(F32)


def front_kernel(
    sz, states, noise, w_t, w_proj, pre_out, hid_out, ext_out, preds_out, w3_out, wt3_out,
    st, ns, wv, xv, pre, preb, hid, ext, preds, w3, wt3v, xs, es, sems,
):
    copies = Copies(sems)
    width = sz.lon
    loads = []
    for m in range(sz.mem):
        loads.append(
            [copies.start(states.at[m], st.at[m]), copies.start(noise.at[m], ns.at[m])]
        )
        if m == 0:
            w_load = copies.start(w_t, wv)
    es[...] = jnp.zeros_like(es)
    taps = 3 * sz.ch
    last = sz.lat // 2 - 1
    stops = (last // 2,)

    def load(m):
        copies.finish(loads[m])
        xs[m] = (st[m].astype(F32) + ns[m]).astype(BF16).astype(F32).reshape(
            sz.ch * sz.lat, sz.lon
        )

    def expand(m, rows):
        for row in rows:
            vals = xs[m, pl.ds(row, sz.ch, stride=sz.lat), :]
            xv[m, :, row * width : (row + 1) * width] = vals
            ext[m, :, (row + 1) * width : (row + 2) * width] = expand_row(vals, es.at[row % 4])

    def rest(m, pair):
        here = slice(pair * 2 * width, (pair + 1) * 2 * width)
        preact = pre[pair % 2]
        preb[m, :, here] = preact.astype(BF16)
        hidden = hidden_pair(preact)
        hid[m, :, here] = hidden
        preds[m, :, here] = project_pair(xv[m, :, here], w_proj, hidden)

    for m in range(sz.mem):
        load(m)
        expand(m, range(5))
        if m == 0:
            copies.finish([w_load])
            for ro in range(3):
                piece = jnp.concatenate(
                    [
                        wv[ro * taps : (ro + 1) * taps, :],
                        jnp.zeros((TAPS - taps, sz.hid), BF16),
                    ],
                    axis=0,
                )
                wt3v[ro] = piece
                w3[:, ro * TAPS : (ro + 1) * TAPS] = piece.T
            copies.start(w3, w3_out)
            copies.start(wt3v, wt3_out)
        pre[1] = conv_pair(sz, ext, w3, m, 1)
        for pair in range(1, last):
            expand(m, range(pair * 2 + 3, min(pair * 2 + 5, sz.lat)) if pair > 1 else ())
            if pair + 1 < last:
                if pair == 1:
                    expand(m, range(5, 7))
                pre[(pair + 1) % 2] = conv_pair(sz, ext, w3, m, pair + 1)
            rest(m, pair)
            if pair == stops[0] or pair + 1 == last:
                first = 1 if pair == stops[0] else stops[0] + 1
                here = slice(first * 2 * width, (pair + 1) * 2 * width)
                copies.start(preb.at[m, :, here], pre_out.at[m, :, here])
                copies.start(hid.at[m, :, here], hid_out.at[m, :, here])
        here = slice(2 * width, sz.pos - 2 * width)
        copies.start(preds.at[m, :, here], preds_out.at[m, :, here])
        inner = slice(width, width + sz.pos)
        copies.start(ext.at[m, :, inner], ext_out.at[m, :, inner])
    copies.finish()


def truth_kernel(sz, target, t_out, xs, ps):
    xs[...] = target[...].astype(F32).reshape(sz.ch * sz.lat, sz.lon)
    if sz.subpad > sz.sub:
        ps[...] = jnp.zeros_like(ps)
    for prow in range(sz.prows):
        for group in range(sz.groups):
            first = prow * 8 + group * sz.parts
            rows = [xs[pl.ds(first + i, sz.ch, stride=sz.lat), :] for i in range(sz.parts)]
            for q, out in enumerate(swap_blocks(rows)):
                ps[q, pl.ds(group * sz.ch, sz.ch), :] = out
        for q in range(sz.parts):
            t_out[prow * sz.parts + q] = ps[q].astype(BF16)


def halo_rows(sz, halos, side):
    band = lax.axis_index("band")
    other = band - 1 if side == 0 else band + 1
    inside = jnp.logical_and(other >= 0, other < sz.bands)
    vals = halos[jnp.clip(other, 0, sz.bands - 1)].astype(F32)
    return vals * jnp.where(inside, 1.0, 0.0)


def rim_kernel(
    sz, halos_in, pre_in, hid_in, ext_in, preds_in, w3_in, w_proj_in,
    pre_out, hid_out, ext_out, snd_out,
    pre, preb, hid, snd, halos, ends, preds, w3, w_proj, xf, rim, es, ps, hr, sems,
):
    width = sz.lon
    copies = Copies(sems)
    load_h = copies.start(halos_in, halos)
    load_w = copies.start(w3_in, w3)
    load_e = []
    for side in range(2):
        at = width if side == 0 else sz.pos - 2 * width
        to = width if side == 0 else 0
        load_e.append(
            copies.start(
                ext_in.at[:, :, at : at + 3 * width], ends.at[side, :, :, to : to + 3 * width]
            )
        )
    load_p = copies.start(w_proj_in, w_proj)
    here = slice(2 * width, sz.pos - 2 * width)
    load_f = [copies.start(preds_in.at[m, :, here], preds.at[m, :, here]) for m in range(sz.mem)]
    es[...] = jnp.zeros_like(es)
    if sz.subpad > sz.sub:
        ps[...] = jnp.zeros_like(ps)
    copies.finish([load_h])
    for side in range(2):
        at = 0 if side == 0 else 3 * width
        hr[side] = halo_rows(sz, halos, side)
        for m in range(sz.mem):
            ends[side, m, :, at : at + width] = expand_row(
                hr[side, pl.ds(m * sz.ch, sz.ch), :], es.at[side * sz.mem + m]
            )
        to = 0 if side == 0 else width + sz.pos
        copies.start(ends.at[side, :, :, at : at + width], ext_out.at[:, :, to : to + width])
    copies.finish([load_w] + load_e)
    last = sz.lat // 2 - 1
    units = [(m, side) for m in range(sz.mem) for side in range(2)]

    def conv(i):
        m, side = units[i]
        pre[i] = conv_pair(sz, ends.at[side], w3, m, 0)

    def rest(i):
        m, side = units[i]
        preact = pre[i]
        preb[i] = preact.astype(BF16)
        hidden = hidden_pair(preact)
        hid[i] = hidden
        xf[i] = ends[side, m, :, width : 3 * width].astype(F32)
        rim[i] = project_pair(xf[i, pl.ds(sz.ch, sz.ch), :], w_proj, hidden)

    def patches(m):
        def row_of(row):
            if row < 2 or row >= sz.lat - 2:
                at = row % 2 * width
                return rim[2 * m if row < 2 else 2 * m + 1, :, at : at + width]
            return preds[m, :, row * width : (row + 1) * width]

        for prow in range(sz.prows):
            for group in range(sz.groups):
                first = prow * 8 + group * sz.parts
                rows = [row_of(first + k) for k in range(sz.parts)]
                for q, out in enumerate(swap_blocks(rows)):
                    ps[m, prow * sz.parts + q, pl.ds(group * sz.ch, sz.ch), :] = out
            for q in range(prow * sz.parts, (prow + 1) * sz.parts):
                snd[m, q] = ps[m, q].astype(BF16)

    copies.finish([load_p] + load_f)
    conv(0)
    for i, (m, side) in enumerate(units):
        if i + 1 < len(units):
            conv(i + 1)
        rest(i)
        if side == 1:
            patches(m)
    for m in range(sz.mem):
        copies.start(snd.at[m], snd_out.at[:, m])
    for i, (m, side) in enumerate(units):
        here = slice(side * last * 2 * width, (side * last + 1) * 2 * width)
        copies.start(preb.at[i], pre_out.at[m, :, here])
        copies.start(hid.at[i], hid_out.at[m, :, here])
    copies.finish()


def slope_kernel(preact, slope):
    rows = 32

    def one(i, carry):
        at = pl.ds(pl.multiple_of(i * rows, rows), rows)
        x = preact[0, at, :].astype(F32)
        twice = 1.0 + lax.erf(x * SQRT_HALF)
        bell = jnp.exp2(x * x * (-0.5 * LOG2_E)) * (2.0 * INV_ROOT_TWO_PI)
        slope[0, at, :] = (twice + x * bell).astype(BF16)
        return carry

    lax.fori_loop(0, preact.shape[1] // rows, one, 0)


def pair_kernel(sz, count, match, preds, truth, grads_out, grads, vals, tsc, sums, scale, inv, sems):
    norm = 1.0 / (32.0 * sz.ch)
    members = sz.members
    folds = sz.subpad // 8
    copies = Copies(sems)
    vals[...] = preds[...].reshape(members, sz.subpad, LANES).astype(F32)
    tsc[...] = truth[lax.axis_index("pair") * 2 + lax.axis_index("core")].astype(F32)

    def squares(diff):
        return jnp.sum((diff * diff).reshape(folds, 8, LANES), axis=0)

    def first(m, carry):
        own = vals[m]
        sums[pl.ds(pl.multiple_of((count * members + m) * 8, 8), 8), :] = squares(own - tsc[...])
        for k in range(count):
            other = match[k, m]
            inv[k, other] = m
            at = pl.multiple_of((k * members + m) * 8, 8)
            sums[pl.ds(at, 8), :] = squares(own - vals[other])
        return carry

    lax.fori_loop(0, members, first, 0, unroll=2)
    rows = (count + 1) * members
    total = sums[pl.ds(0, rows, stride=8), :]
    for j in range(1, 8):
        total = total + sums[pl.ds(j, rows, stride=8), :]
    step = sz.lon // sz.parts
    while step < LANES:
        total = total + pltpu.roll(total, step, 1)
        step *= 2
    lane = lax.broadcasted_iota(jnp.int32, total.shape, 1)
    for bit in (1, 2):
        total = total + jnp.where(
            (lane & bit) == 0, pltpu.roll(total, LANES - bit, 1), pltpu.roll(total, bit, 1)
        )
    inverse = lax.rsqrt(total * norm + 1e-06)
    scale[pl.ds(0, count * members), :] = inverse[: count * members] * (0.5 / count)
    scale[pl.ds(count * members, members), :] = inverse[count * members :]

    def second(m):
        weight = scale[pl.ds(count * members + m, 1), :]
        acc = None
        own_weight = weight
        for k in range(count):
            back = inv[k, m]
            for other, index in ((match[k, m], k * members + m), (back, k * members + back)):
                part = scale[pl.ds(index, 1), :]
                own_weight = own_weight - part
                term = part * vals[other]
                acc = term if acc is None else acc + term
        return (own_weight * vals[m] + (acc - weight * tsc[...])).astype(BF16)

    quarter = sz.devs // 4
    for part in range(4):

        def several(i, carry):
            m = part * (members // 4) + i
            grads[m // sz.mem, m % sz.mem] = second(m)
            return carry

        lax.fori_loop(0, members // 4, several, 0, unroll=2)
        at = slice(part * quarter, (part + 1) * quarter)
        copies.start(grads.at[at], grads_out.at[at])
    copies.finish()


def fold_taps(part, channels):
    return (
        part[channels : 2 * channels]
        + shift_left(part[0:channels])
        + shift_right(part[2 * channels : 3 * channels])
    )


def weight_sums(sz, core, gpre, hid_half, ext, gp, store):
    block = sz.hid // sz.devs

    def take(ref):
        rows = []
        for z in range(sz.devs // 2):
            at = pl.ds(pl.multiple_of((2 * z + core) * block, block), block)
            rows.append(jnp.concatenate([ref[m, at, :] for m in range(sz.mem)], axis=1))
        return jnp.concatenate(rows, axis=0)

    dims = (((1,), (1,)), ((), ()))
    left = take(gpre)
    for ro in range(3):
        cols = [ext[m, :, ro * sz.lon : ro * sz.lon + sz.pos] for m in range(sz.mem)]
        store(
            ro * TAPS,
            lax.dot_general(
                left, jnp.concatenate(cols, axis=1), dims, preferred_element_type=F32
            ),
        )
    cols = [gp[m] for m in range(sz.mem)]
    store(
        3 * TAPS,
        0.5
        * lax.dot_general(
            jnp.concatenate([hid_half[m] for m in range(sz.mem)], axis=1),
            jnp.concatenate(cols, axis=1),
            dims,
            preferred_element_type=F32,
        ),
    )
    store(sz.used, jnp.zeros((sz.hid // 2, sz.cols - sz.used), F32))


def sibling_kernel(
    sz, back_in, slope_in, hid_in, ext, w_proj, gp, gpre, hid, sib,
    back, slope, hid_sib, rows_f, wpt, sems,
):
    width = sz.lon
    copies = Copies(sems)
    load_b = copies.start(back_in, back)
    load_s = [copies.start(slope_in.at[m], slope.at[m]) for m in range(sz.mem)]
    block = sz.hid // sz.devs
    mine = lax.axis_index("core")
    load_h = []
    for half, core in ((hid_sib, 1 - mine), (hid, mine)):
        for m in range(sz.mem):
            for z in range(sz.devs // 2):
                at = pl.ds(pl.multiple_of((2 * z + core) * block, block), block)
                to = slice(z * block, (z + 1) * block)
                load_h.append(copies.start(hid_in.at[m, at, :], half.at[m, to, :]))
    wpt[...] = (w_proj[...].astype(F32) * 0.5).T.astype(BF16)
    copies.finish([load_b])
    for m in range(sz.mem):
        for prow in range(sz.prows):
            parts = range(prow * sz.parts, (prow + 1) * sz.parts)
            for q in parts:
                rows_f[m, q] = back[q, m].astype(F32)
            for group in range(sz.groups):
                outs = swap_blocks([rows_f[m, q, pl.ds(group * sz.ch, sz.ch), :] for q in parts])
                for i, out in enumerate(outs):
                    row = prow * 8 + group * sz.parts + i
                    gp[m, :, row * width : (row + 1) * width] = out.astype(BF16)
        for pair in range(sz.lat // 2):
            here = slice(pair * 2 * width, (pair + 1) * 2 * width)
            if pair == 0:
                copies.finish([load_s[m]])
            dhid = jnp.dot(wpt[...], gp[m, :, here], preferred_element_type=F32)
            gpre[m, :, here] = (dhid * slope[m, :, here].astype(F32)).astype(BF16)
    def store(at, term):
        sib[:, at : at + term.shape[1]] = term.astype(BF16)

    copies.finish(load_h[: len(load_h) // 2])
    weight_sums(sz, 1 - mine, gpre, hid_sib, ext, gp, store)
    copies.finish()


def own_kernel(sz, gpre, hid, ext, gp, wt3, own, edge_up, edge_dn):
    def store(at, term):
        own[:, at : at + term.shape[1]] = term

    weight_sums(sz, lax.axis_index("core"), gpre, hid, ext, gp, store)
    for side, edge in enumerate((edge_up, edge_dn)):
        at = 0 if side == 0 else sz.pos - sz.lon
        cols = [gpre[m, :, at : at + sz.lon] for m in range(sz.mem)]
        part = jnp.dot(
            wt3[2 * side], jnp.concatenate(cols, axis=1), preferred_element_type=F32
        )
        for m in range(sz.mem):
            edge[m] = fold_taps(part[:, m * sz.lon : (m + 1) * sz.lon], sz.ch)


def merge_kernel(own, other, out):
    out[...] = (own[...] + other[...].astype(F32)).astype(BF16)


def data_kernel(sz, gpre_in, gp_in, wt3_in, ov, ev, gpre, gp, wt3, gs, sems):
    width = sz.lon
    copies = Copies(sems)
    load_w = copies.start(wt3_in, wt3)
    half = sz.pos // 2
    loads, load_p = [], []
    for m in range(sz.mem):
        for part in range(2):
            at = slice(part * half, (part + 1) * half)
            loads.append(copies.start(gpre_in.at[m, :, at], gpre.at[m, :, at]))
            if part == 0:
                load_p.append(copies.start(gp_in.at[m], gp.at[m]))
    zero = jnp.zeros((sz.hid, width), BF16)
    copies.finish([load_w])
    for m in range(sz.mem):
        copies.finish(loads[2 * m : 2 * m + 2] + [load_p[m]])

        def two_rows(first):
            low, high = max(first, 0), min(first + 2, sz.lat)
            cols = [gpre[m, :, low * width : high * width]]
            if first < 0:
                cols.insert(0, zero)
            if first + 2 > sz.lat:
                cols.append(zero)
            return cols[0] if len(cols) == 1 else jnp.concatenate(cols, axis=1)

        for pair in range(sz.lat // 2):
            part = None
            for ro in range(3):
                term = jnp.dot(wt3[ro], two_rows(pair * 2 + 1 - ro), preferred_element_type=F32)
                part = term if part is None else part + term
            for i in range(2):
                row = pair * 2 + i
                at = row * width
                total = gp[m, :, at : at + width].astype(F32) + fold_taps(
                    part[:, i * width : (i + 1) * width], sz.ch
                )
                if row in (0, sz.lat - 1):
                    ev[0 if row == 0 else 1, m] = total
                gs[pl.ds(row, sz.ch, stride=sz.lat), :] = total
        ov[m] = gs[...].reshape(sz.ch, sz.lat, width).astype(BF16)


def border_kernel(sz, part, ev, uv, dv, out, ov, gs, sems):
    width = sz.lon
    copies = Copies(sems)
    for m in range(sz.mem):
        gs[...] = part[m].astype(F32).reshape(sz.ch * sz.lat, width)
        gs[pl.ds(0, sz.ch, stride=sz.lat), :] = ev[0, m] + uv[m]
        gs[pl.ds(sz.lat - 1, sz.ch, stride=sz.lat), :] = ev[1, m] + dv[m]
        ov[m] = gs[...].reshape(sz.ch, sz.lat, width).astype(BF16)
        copies.start(ov.at[m], out.at[m])
    copies.finish()


def final_kernel(sz, factor, terms, conv, proj):
    total = terms[0].astype(F32)
    for i in range(1, terms.shape[0]):
        total = total + terms[i].astype(F32)
    total = total * factor
    taps = 3 * sz.ch
    for ro in range(3):
        conv[:, ro * taps : (ro + 1) * taps] = total[:, ro * TAPS : ro * TAPS + taps]
    proj[...] = total[:, 3 * TAPS : sz.used]


MEMBER = ("pair", "core")


def on_device(states, noise_field, target, w_conv, w_proj, matchings):
    member_count = lax.axis_size("pair") * lax.axis_size("core")
    band_count = lax.axis_size("band")
    sz = Sizes(states, w_conv, member_count, band_count)
    mem, ch, lat, lon, hid, pos = sz.mem, sz.ch, sz.lat, sz.lon, sz.hid, sz.pos
    count = matchings.shape[0]
    down = [(i, i + 1) for i in range(band_count - 1)]
    up = [(i + 1, i) for i in range(band_count - 1)]
    ext_shape = (mem, TAPS, pos + 2 * lon)
    part_shape = (sz.devs, mem, sz.subpad, LANES)
    flat = pltpu.VMEM((ch * lat, lon), F32)
    taps_row = pltpu.VMEM((TAPS, lon), F32)
    regroup_rows = pltpu.VMEM((sz.parts, sz.subpad, LANES), F32)
    wide_bf = pltpu.VMEM((mem, hid, pos), BF16)
    halo_shape = (band_count, mem * ch, lon)

    both_bf = pltpu.VMEM((mem, ch, lat, lon), BF16)
    both_f = pltpu.VMEM((mem, ch, lat, lon), F32)
    (send,) = call(
        functools.partial(edges_kernel, sz),
        "edges",
        [(halo_shape, BF16)],
        [
            both_bf,
            both_f,
            pltpu.VMEM((ch * 8, lon), F32),
            pltpu.VMEM(halo_shape, BF16),
            pltpu.VMEM((2, mem * ch, lon), F32),
            dma(2 * mem + 1),
        ],
        1_000_000,
        3_000_000,
        (states, noise_field),
    )
    halos = lax.all_to_all(send, "band", 0, 0, tiled=True)
    conv_flops = 2 * mem * pos * hid * 3 * TAPS
    wide = (mem, hid, pos)
    pair_shape = (hid, 2 * lon)
    preact, hidden, ext, fields, w3, wt3 = call(
        functools.partial(front_kernel, sz),
        "front",
        [
            (wide, BF16),
            (wide, BF16),
            (ext_shape, BF16),
            ((mem, ch, pos), F32),
            ((hid, 3 * TAPS), BF16),
            ((3, TAPS, hid), BF16),
        ],
        [
            both_bf,
            both_f,
            pltpu.VMEM((9 * ch, hid), BF16),
            pltpu.VMEM((mem, ch, pos), F32),
            pltpu.VMEM((2,) + pair_shape, F32),
            wide_bf,
            wide_bf,
            pltpu.VMEM(ext_shape, BF16),
            pltpu.VMEM((mem, ch, pos), F32),
            pltpu.VMEM((hid, 3 * TAPS), BF16),
            pltpu.VMEM((3, TAPS, hid), BF16),
            pltpu.VMEM((mem, ch * lat, lon), F32),
            pltpu.VMEM((4, TAPS, lon), F32),
            dma(3 + 4 * mem + mem * lat // 2),
        ],
        conv_flops,
        9_000_000,
        (states, noise_field, w_conv.T, w_proj),
        vmem=(3,),
        limit=55,
    )
    units = 2 * mem
    preact, hidden, ext, snd = call(
        functools.partial(rim_kernel, sz),
        "rim",
        [(wide, BF16), (wide, BF16), (ext_shape, BF16), (part_shape, BF16)],
        [
            pltpu.VMEM((units,) + pair_shape, F32),
            pltpu.VMEM((units,) + pair_shape, BF16),
            pltpu.VMEM((units,) + pair_shape, BF16),
            pltpu.VMEM((mem, sz.devs, sz.subpad, LANES), BF16),
            pltpu.VMEM(halo_shape, BF16),
            pltpu.VMEM((2, mem, TAPS, 4 * lon), BF16),
            pltpu.VMEM((mem, ch, pos), F32),
            pltpu.VMEM((hid, 3 * TAPS), BF16),
            pltpu.VMEM(w_proj.shape, BF16),
            pltpu.VMEM((units, TAPS, 2 * lon), F32),
            pltpu.VMEM((units, ch, 2 * lon), F32),
            pltpu.VMEM((units, TAPS, lon), F32),
            pltpu.VMEM((mem, sz.devs, sz.subpad, LANES), F32),
            pltpu.VMEM((2, mem * ch, lon), F32),
            dma(7 + 2 * units + 2 * mem),
        ],
        conv_flops // 4,
        9_000_000,
        (halos, preact, hidden, ext, fields, w3, w_proj),
        limit=53,
        aliases={1: 0, 2: 1, 3: 2},
    )

    preds = lax.all_to_all(snd, MEMBER, 0, 0, tiled=True)
    late_target, _ = lax.optimization_barrier((target, snd))
    (truth,) = call(
        functools.partial(truth_kernel, sz),
        "truth",
        [((sz.devs, sz.subpad, LANES), BF16)],
        [flat, regroup_rows],
        5_000_000,
        2_000_000,
        (late_target,),
        vmem=(0,),
        vmem_outs=(0,),
        limit=16,
    )
    block = pl.BlockSpec((1, hid // 4, pos), lambda m, i: (m, i, 0))
    slope = pl.pallas_call(
        slope_kernel,
        grid=(mem, 4),
        in_specs=[block],
        out_specs=block,
        out_shape=jax.ShapeDtypeStruct((mem, hid, pos), BF16),
        compiler_params=pltpu.CompilerParams(vmem_limit_bytes=40 * 1024 * 1024),
        cost_estimate=pl.CostEstimate(
            flops=10 * mem * hid * pos, bytes_accessed=8 * mem * hid * pos, transcendentals=0
        ),
        name="slope",
    )(preact)

    rows = (count + 1) * sz.members
    (grads,) = call(
        functools.partial(pair_kernel, sz, count),
        "pairs",
        [(part_shape, BF16)],
        [
            pltpu.VMEM(part_shape, BF16),
            pltpu.VMEM((sz.members, sz.subpad, LANES), F32),
            pltpu.VMEM((sz.subpad, LANES), F32),
            pltpu.VMEM((rows * 8, LANES), F32),
            pltpu.VMEM((rows, LANES), F32),
            pltpu.SMEM((count, sz.members), jnp.int32),
            dma(4),
        ],
        sz.members * 30 * sz.subpad * LANES,
        2_000_000,
        (matchings, preds, truth),
        smem=(0,),
        vmem=(1, 2),
        limit=16,
    )
    back = lax.all_to_all(grads, MEMBER, 0, 0, tiled=True)

    half = (hid // 2, sz.cols)
    edge_shape = (mem, ch, lon)
    grad_pred, grad_pre, hid_own, sibling = call(
        functools.partial(sibling_kernel, sz),
        "sibling",
        [
            ((mem, ch, pos), BF16),
            ((mem, hid, pos), BF16),
            ((mem, hid // 2, pos), BF16),
            (half, BF16),
        ],
        [
            pltpu.VMEM(part_shape, BF16),
            pltpu.VMEM((mem, hid, pos), BF16),
            pltpu.VMEM((mem, hid // 2, pos), BF16),
            pltpu.VMEM((mem, sz.devs, sz.subpad, LANES), F32),
            pltpu.VMEM((hid, ch), BF16),
            dma(1 + mem + mem * sz.devs),
        ],
        conv_flops,
        9_000_000,
        (back, slope, hidden, ext, w_proj),
        vmem=(0, 3, 4),
        vmem_outs=range(4),
        limit=40,
    )
    swapped = lax.ppermute(sibling, "core", [(0, 1), (1, 0)])
    own, edge_up, edge_dn = call(
        functools.partial(own_kernel, sz),
        "own",
        [(half, F32), (edge_shape, F32), (edge_shape, F32)],
        [],
        conv_flops // 2,
        9_000_000,
        (grad_pre, hid_own, ext, grad_pred, wt3),
        vmem=range(5),
        vmem_outs=range(3),
        limit=16,
    )
    (partial,) = call(
        merge_kernel,
        "merge",
        [(half, BF16)],
        [],
        500_000,
        2_000_000,
        (own, swapped),
        vmem=(0, 1),
        vmem_outs=(0,),
        limit=16,
    )
    shards = member_count * band_count
    each = hid // shards
    terms = lax.all_to_all(
        partial.reshape(shards // 2, each, sz.cols), ("pair", "band"), 0, 0, tiled=True
    )
    edge_up, edge_dn, late_wt3, _ = lax.optimization_barrier((edge_up, edge_dn, wt3, partial))
    from_dn = lax.ppermute(edge_up, "band", up)
    from_up = lax.ppermute(edge_dn, "band", down)

    part_states, edge_sums = call(
        functools.partial(data_kernel, sz),
        "data",
        [((mem, ch, lat, lon), BF16), ((2,) + edge_shape, F32)],
        [
            wide_bf,
            pltpu.VMEM((mem, ch, pos), BF16),
            pltpu.VMEM((3, TAPS, hid), BF16),
            flat,
            dma(1 + 3 * mem),
        ],
        conv_flops,
        8_000_000,
        (grad_pre, grad_pred, late_wt3),
        vmem_outs=(0, 1),
        limit=50,
    )
    (grad_states,) = call(
        functools.partial(border_kernel, sz),
        "border",
        [((mem, ch, lat, lon), BF16)],
        [
            pltpu.VMEM((mem, ch, lat, lon), BF16),
            flat,
            dma(mem),
        ],
        1_000_000,
        2_000_000,
        (part_states, edge_sums, from_up, from_dn),
        vmem=range(4),
        limit=16,
    )

    factor = 1.0 / (pos * sz.members * band_count) ** 0.5
    grad_conv, grad_proj = call(
        functools.partial(final_kernel, sz, factor),
        "final",
        [((each, 9 * ch), F32), ((each, ch), F32)],
        [],
        500_000,
        500_000,
        (terms,),
        vmem=(0,),
        vmem_outs=(0, 1),
        limit=16,
    )
    return grad_states, grad_conv, grad_proj.T


def solution(mesh):
    members = mesh.shape["member"]
    split = jax.sharding.Mesh(
        mesh.devices.reshape(members // 2, 2, mesh.shape["band"]), MEMBER + ("band",)
    )
    return jax.shard_map(
        on_device,
        mesh=split,
        in_specs=(
            P(MEMBER, None, "band", None),
            P(MEMBER, None, "band", None),
            P(None, "band", None),
            P(),
            P(),
            P(),
        ),
        out_specs=(
            P(MEMBER, None, "band", None),
            P(MEMBER + ("band",), None),
            P(None, MEMBER + ("band",)),
        ),
        check_vma=False,
    )
```
